768 devices in a mesh: dp: 32 (over x, y), member: 2 (over core), expert: 12 (over z).
Axes of the slice: x: 4, y: 8, z: 12, core: 2. Of those that a mesh axis runs over, the one named last changes fastest.
Arguments:
- tokens: bfloat16 [8192, 1280], P(('dp', 'member')), may hold values from -6 to 6
- route_ids: int32 [2, 8192, 1], P(None, ('dp', 'member')), may hold values from 0 to 31; in each aligned block of 128 rows (0 to 127, 128 to 255, ..., all dimensions but the last counted through in order) at most 6 rows name the same one
- router: float32 [2, 1280, 32], replicated, may hold values from -0.15625 to 0.15625
- w_in: bfloat16 [2, 32, 1280, 4608], P('member', 'dp', None, 'expert'), may hold values from -0.15625 to 0.15625
- w_out: bfloat16 [2, 32, 4608, 1280], P('member', 'dp', 'expert'), may hold values from -0.09375 to 0.09375
- out_grad: bfloat16 [2, 8192, 1280], P(None, ('dp', 'member')), may hold values from -6 to 6
Outputs:
- moe_out: bfloat16 [2, 8192, 1280], P(None, ('dp', 'member'))
- token_grad: float32 [8192, 1280], P(('dp', 'member'))
- first_grad: bfloat16 [2, 32, 1280, 4608], P('member', 'dp', None, 'expert')
- second_grad: bfloat16 [2, 32, 4608, 1280], P('member', 'dp', 'expert')
- router_grad: float32 [2, 1280, 32], replicated
The draws below stay inside these ranges and needn't reach their ends.
Inputs may be any that keep to these rules, and one draw needn't show every extreme that they name: `route_ids`: in each aligned block of 128 rows of one member no expert is named by more than 6 rows, and some block names some expert exactly 6 times.
All inputs are finite; a program needn't handle non-finite values.
Results may differ from the reference program's by a relative error of at most 0.022.
Values may be sent and summed in bfloat16 or wider, within the bound.
No kernel may reach another device: no remote copies, remote signals or barrier semaphores. Data moves between devices by JAX's collectives and lax.ppermute only.
A program may use at most 64 MiB of HBM per device.

```python
import math
import jax
import jax.numpy as jnp
import numpy as np
from jax import lax

D = 1280
HID = 4608
TOK_DEV = 128
MEMBERS = 2
EXPERTS = 32
TOKENS = 8192
CAP = 6
N_EXPERT = 12


def block_levels(key, shape, cuts, low, top_value):
    level, own = 1.0, jax.random.fold_in(key, 6)
    for position, blocks in cuts:
        steps = jnp.exp(jax.random.uniform(jax.random.fold_in(own, position), (blocks,), jnp.float32, low / len(cuts), top_value / len(cuts)))
        level = level * jnp.repeat(steps, shape[position] // blocks).reshape([-1 if axis == position else 1 for axis in range(len(shape))])
    return level


def shared_out(rng, own, number, rows, amount, top, bound, slope):
    sequence = jax.random.permutation(rng, amount)
    crowded, ordinary = portions_of(amount, rows * top, bound, slope, True), portions_of(amount, rows * top, bound, slope, False)
    places = jnp.arange(amount)

    def named(sizes, rotation):
        used = int((sizes > 0).sum())
        fixed = max(1, used // 4)
        shifted = fixed + (places - fixed + rotation * (used - fixed)) % max(1, amount - fixed)
        return jnp.zeros((amount,), jnp.int32).at[sequence[jnp.where(places < fixed, places, shifted)]].set(jnp.asarray(sizes, jnp.int32))

    sizes = jnp.where(number % 4 == 0, named(crowded, number // 4), named(ordinary, number - number // 4 - 1))
    mixed = jax.random.permutation(jax.random.fold_in(own, 3), amount)
    donor, receiver = mixed[0:amount // 2 * 2:2], mixed[1:amount // 2 * 2:2]
    slack = jnp.minimum(sizes[donor] - 1, bound - sizes[receiver]) // 2
    slack = jnp.where((donor == sequence[0]) | (receiver == sequence[0]) | (sizes[receiver] == 0), 0, jnp.maximum(slack, 0))
    shifted = jax.random.randint(jax.random.fold_in(own, 4), (amount // 2,), 0, 1 << 20) % (slack + 1)
    sizes = sizes.at[donor].add(-shifted).at[receiver].add(shifted)
    labels = jnp.searchsorted(jnp.cumsum(sizes), jnp.arange(rows * top), side="right").astype(jnp.int32)
    grid = labels.reshape(top, rows).T
    grid = grid[jax.random.permutation(jax.random.fold_in(own, 1), rows)]
    rotation = jax.random.randint(jax.random.fold_in(own, 2), (rows, 1), 0, top)
    return jnp.take_along_axis(grid, (jnp.arange(top)[None, :] + rotation) % top, axis=1)


def portions_of(amount, total, bound, skew, full):
    weights = [(1 << 20) // math.isqrt(grade ** skew) + 1 for grade in range(1, amount + 1)]
    largest = bound if full else min(bound, max(-(-total // amount), total * weights[0] // sum(weights)))
    least = 1 if total - largest >= amount - 1 else 0
    given, spare = [largest] + [least] * (amount - 1), total - largest - least * (amount - 1)
    while spare > 0:
        free = [i for i in range(1, amount) if given[i] < largest] or [i for i in range(1, amount) if given[i] < bound]
        pool, remaining = sum([weights[i] for i in free]), spare
        for i in free:
            extra = min(bound - given[i], max(1, remaining * weights[i] // pool), spare)
            given[i] = given[i] + extra
            spare = spare - extra
    return np.array(given)


def scatter_about(key, dims, spread, limit, shards=(), held_as=jnp.bfloat16):
    entries = spread * jax.random.normal(key, dims, jnp.float32)
    if shards:
        entries = entries * block_levels(key, dims, shards, -0.22, 0.18)
    return jnp.clip(entries, -limit, limit).astype(held_as)


def setup_inputs(seed: int = 0) -> dict:
    streams_of = jax.random.split(jax.random.key(seed), 7)
    tokens = scatter_about(streams_of[0], (TOKENS, D), 1.0, 6.0, ((0, 64),))
    route_ids_keys = jax.random.split(jax.random.fold_in(streams_of[1], 1), MEMBERS * TOKENS // TOK_DEV)
    route_ids_turns = jax.random.permutation(jax.random.fold_in(streams_of[1], 3), MEMBERS * TOKENS // TOK_DEV)
    route_ids = jax.vmap(lambda own, number: shared_out(jax.random.fold_in(streams_of[1], 2), own, number, TOK_DEV, EXPERTS, 1, CAP, 2))(route_ids_keys, route_ids_turns).reshape((MEMBERS, TOKENS, 1))
    router = scatter_about(streams_of[2], (MEMBERS, D, EXPERTS), D ** -0.5, 0.15625, (), jnp.float32)
    w_in = scatter_about(streams_of[3], (MEMBERS, EXPERTS, D, HID), D ** -0.5, 0.15625, ((0, 2), (1, 32), (3, 12)))
    w_out = scatter_about(streams_of[4], (MEMBERS, EXPERTS, HID, D), HID ** -0.5, 0.09375, ((0, 2), (1, 32), (2, 12)))
    out_grad = scatter_about(streams_of[5], (MEMBERS, TOKENS, D), 1.0, 6.0, ((1, 64),))
    return dict(tokens=tokens, route_ids=route_ids, router=router, w_in=w_in, w_out=w_out, out_grad=out_grad)


tanh_scale = 0.7978845608028654
cubic_term = 0.044715


def gelu_pair(pre_act):
    inner = tanh_scale * (pre_act + cubic_term * pre_act * pre_act * pre_act)
    tanh_value = jnp.tanh(inner)
    value = 0.5 * pre_act * (1.0 + tanh_value)
    gelu_slope = 0.5 * (1.0 + tanh_value) + 0.5 * pre_act * (1.0 - tanh_value * tanh_value) * tanh_scale * (1.0 + 3.0 * cubic_term * pre_act * pre_act)
    return value, gelu_slope


def slot_rank(expert_ids, experts):
    hot_table = (expert_ids[..., None] == jnp.arange(experts, dtype=jnp.int32)).astype(jnp.int32)
    earlier = jnp.cumsum(hot_table, axis=-2) - hot_table
    return jnp.sum(earlier * hot_table, axis=-1).astype(jnp.int32)


def expert_pass(operands):
    x_rows, g_rows, w_first, w_second = operands
    row_count = x_rows.shape[0]
    pre_act = jnp.dot(x_rows, w_first, preferred_element_type=jnp.float32)
    act_value, gelu_slope = gelu_pair(pre_act)
    activation = act_value.astype(jnp.bfloat16)
    hidden_grad = jnp.dot(g_rows, w_second.T, preferred_element_type=jnp.float32)
    pre_grad = (hidden_grad * gelu_slope).astype(jnp.bfloat16)
    grad_first = jnp.dot(x_rows.T, pre_grad, preferred_element_type=jnp.float32)
    grad_second = jnp.dot(activation.T, g_rows, preferred_element_type=jnp.float32)
    block_width = HID // N_EXPERT
    act_blocks = activation.astype(jnp.float32).reshape(row_count, N_EXPERT, block_width)
    second_blocks = w_second.astype(jnp.float32).reshape(N_EXPERT, block_width, D)
    part_out = jnp.einsum("rjh,jhd->jrd", act_blocks, second_blocks, precision=lax.Precision.HIGHEST).astype(jnp.bfloat16)
    out_rows = jnp.sum(part_out.astype(jnp.float32), axis=0).astype(jnp.bfloat16)
    grad_blocks = pre_grad.astype(jnp.float32).reshape(row_count, N_EXPERT, block_width)
    first_blocks = w_first.astype(jnp.float32).reshape(D, N_EXPERT, block_width)
    part_dx = jnp.einsum("rjh,djh->jrd", grad_blocks, first_blocks, precision=lax.Precision.HIGHEST).astype(jnp.bfloat16)
    dx_rows = jnp.sum(part_dx.astype(jnp.float32), axis=0).astype(jnp.bfloat16)
    return out_rows, dx_rows, grad_first, grad_second


def reference(tokens, route_ids, router, w_in, w_out, out_grad):
    sources = TOKENS // TOK_DEV
    buffer_rows = sources * CAP
    expert_ids = route_ids[:, :, 0]
    slot_rows = slot_rank(expert_ids.reshape(MEMBERS, sources, TOK_DEV), EXPERTS).reshape(MEMBERS, TOKENS)
    block_index = (jnp.arange(TOKENS, dtype=jnp.int32) // TOK_DEV).astype(jnp.int32)
    tokens_f = tokens.astype(jnp.float32)
    hot_table = (expert_ids[..., None] == jnp.arange(EXPERTS, dtype=jnp.int32)).astype(jnp.float32)
    logits = jnp.einsum("td,mde->mte", tokens_f, router, precision=lax.Precision.HIGHEST)
    gate_value = jax.nn.sigmoid(jnp.sum(logits * hot_table, axis=-1))
    scaled = (gate_value[..., None] * out_grad.astype(jnp.float32)).astype(jnp.bfloat16)
    token_grad = jnp.zeros((TOKENS, D), jnp.float32)
    moe_list = []
    first_list = []
    second_list = []
    router_list = []
    for member in range(MEMBERS):
        buffer_index = (expert_ids[member] * buffer_rows + block_index * CAP + slot_rows[member]).astype(jnp.int32)
        x_rows = jnp.zeros((EXPERTS * buffer_rows, D), jnp.bfloat16).at[buffer_index].set(tokens).reshape(EXPERTS, buffer_rows, D)
        g_rows = jnp.zeros((EXPERTS * buffer_rows, D), jnp.bfloat16).at[buffer_index].set(scaled[member]).reshape(EXPERTS, buffer_rows, D)
        out_rows, dx_rows, grad_first, grad_second = lax.map(expert_pass, (x_rows, g_rows, w_in[member], w_out[member]))
        expert_output = out_rows.reshape(EXPERTS * buffer_rows, D)[buffer_index]
        expert_dx = dx_rows.reshape(EXPERTS * buffer_rows, D)[buffer_index]
        moe_list.append((gate_value[member][:, None] * expert_output.astype(jnp.float32)).astype(jnp.bfloat16))
        gate_grad = jnp.sum(out_grad[member].astype(jnp.float32) * expert_output.astype(jnp.float32), axis=-1)
        logit_grad = gate_grad * gate_value[member] * (1.0 - gate_value[member])
        weighted = hot_table[member] * logit_grad[:, None]
        router_list.append(jnp.dot(tokens_f.T, weighted, precision=lax.Precision.HIGHEST))
        token_grad = token_grad + expert_dx.astype(jnp.float32) + jnp.dot(weighted, router[member].T, precision=lax.Precision.HIGHEST)
        first_list.append(grad_first.astype(jnp.bfloat16))
        second_list.append(grad_second.astype(jnp.bfloat16))
    return (jnp.stack(moe_list), token_grad, jnp.stack(first_list), jnp.stack(second_list), jnp.stack(router_list))
```

```python
import functools

import jax
import jax.numpy as jnp
from jax import lax
from jax.experimental import pallas as pl
from jax.experimental.pallas import tpu as pltpu
from jax.sharding import PartitionSpec as P

BF = jnp.bfloat16
F32 = jnp.float32
tanh_scale = 0.7978845608028654
cubic_term = 0.044715
LIMIT = 44 << 20
VM = pl.BlockSpec(memory_space=pltpu.VMEM)
SM = pl.BlockSpec(memory_space=pltpu.SMEM)


def iota(shape, axis):
    return lax.broadcasted_iota(jnp.int32, shape, axis)


def one(mask):
    return jnp.where(mask, 1.0, 0.0).astype(BF)


def to_column(row):
    n = row.shape[1]
    eye = iota((n, n), 0) == iota((n, n), 1)
    return jnp.sum(jnp.where(eye, row, 0), axis=1, keepdims=True)


def dispatch_kernel(ids_ref, tok_ref, grad_ref, msg_ref, code_ref):
    tok_rows, width = tok_ref.shape
    half = width // 2
    codes = []
    for m in range(2):
        ids = ids_ref[m : m + 1, :]
        same = to_column(ids) == ids
        earlier = iota((tok_rows, tok_rows), 0) < iota((tok_rows, tok_rows), 1)
        slot = jnp.sum(jnp.where(same & earlier, 1, 0), axis=0, keepdims=True)
        code = ids * 8 + slot
        code_ref[m : m + 1, :] = code
        codes.append(code)
    sides = [
        jnp.concatenate([v[:, :half], v[:, half:]], axis=0)
        for v in (tok_ref[...], grad_ref[0], grad_ref[1])
    ]
    block = 256
    for b in range(msg_ref.shape[0] // block):
        row = iota((block, tok_rows), 0) + b * block
        dest = lax.shift_right_logical(row * 2731, 16)
        rest = row - dest * 24
        slot = 2 * lax.shift_right_logical(rest, 3) + (rest & 1)
        kind = lax.shift_right_logical(rest & 7, 1)
        code = lax.shift_right_logical(dest, 1) * 8 + slot
        member = dest & 1
        hit0 = (code == codes[0]) & (member == 0)
        hit1 = (code == codes[1]) & (member == 1)
        hit = hit0 | hit1
        parts = (
            [hit & (kind == 0), hit & (kind == 1)],
            [hit0 & (kind == 2), hit0 & (kind == 3)],
            [hit1 & (kind == 2), hit1 & (kind == 3)],
        )
        total = None
        for pair, side in zip(parts, sides):
            pick = jnp.concatenate([one(p) for p in pair], axis=1)
            term = jnp.dot(pick, side, preferred_element_type=F32)
            total = term if total is None else total + term
        msg_ref[pl.ds(b * block, block), :] = total.astype(BF)


def nt(a, b):
    return lax.dot_general(a, b, (((1,), (1,)), ((), ())), preferred_element_type=F32)


def tn(a, b):
    return lax.dot_general(a, b, (((0,), (0,)), ((), ())), preferred_element_type=F32)


def expert_kernel(
    stride, msg_ref, first_ref, second_ref, router_ref, part_ref, x_ref, g_ref, pre_ref, act_ref
):
    rows, width = x_ref.shape
    half = width // 2
    chunks = width // 128
    first = first_ref[...]
    second = second_ref[...]
    router = router_ref[...]
    p = iota((256, 256), 0)
    source = (
        lax.shift_right_logical(p & 63, 1) * 8 + lax.shift_right_logical(p, 6) * 2 + (p & 1)
    )
    sort = one(source == iota((256, 256), 1))
    router_sum = jnp.zeros((1, width), F32)
    block = 128
    for b in range(rows // block):
        for k in range(2):
            part = jnp.dot(
                sort, msg_ref[pl.ds((2 * b + k) * 256, 256), :], preferred_element_type=F32
            ).astype(BF)
            here = pl.ds(b * block + k * 64, 64)
            x_ref[here, 0:half] = part[0:64]
            x_ref[here, half:width] = part[64:128]
            g_ref[here, 0:half] = part[128:192]
            g_ref[here, half:width] = part[192:256]
        here = pl.ds(b * block, block)
        x = x_ref[here, :]
        g = g_ref[here, :]
        xf = x.astype(F32)
        logit = jnp.sum(xf * router, axis=1, keepdims=True)
        gate = 1.0 / (1.0 + jnp.exp(-logit))
        pre = jnp.dot(x, first, preferred_element_type=F32)
        hidden = nt(g, second)
        tanh_value = jnp.tanh(tanh_scale * (pre + cubic_term * pre * pre * pre))
        act = 0.5 * pre * (1.0 + tanh_value)
        slope = 0.5 * (1.0 + tanh_value) + 0.5 * pre * (
            1.0 - tanh_value * tanh_value
        ) * tanh_scale * (1.0 + 3.0 * cubic_term * pre * pre)
        gate_grad = jnp.sum(act * hidden, axis=1, keepdims=True)
        logit_grad = gate_grad * gate * (1.0 - gate)
        pre_grad = (hidden * gate * slope).astype(BF)
        scaled_act = (act * gate).astype(BF)
        pre_ref[here, :] = pre_grad
        act_ref[here, :] = scaled_act
        router_sum = router_sum + jnp.sum(xf * logit_grad, axis=0, keepdims=True)
        out = jnp.dot(scaled_act, second, preferred_element_type=F32).astype(BF)
        dx = (nt(pre_grad, first) + logit_grad * router).astype(BF)
        for c in range(chunks):
            lanes = slice(c * 128, (c + 1) * 128)
            part_ref[pl.ds(c * stride + b * block, block), :] = out[:, lanes]
            part_ref[pl.ds(c * stride + rows + b * block, block), :] = dx[:, lanes]
    for c in range(chunks):
        lanes = slice(c * 128, (c + 1) * 128)
        tail = jnp.where(iota((16, 128), 0) == 0, router_sum[:, lanes], 0.0)
        part_ref[pl.ds(c * stride + 2 * rows, 16), :] = tail.astype(BF)
    left = part_ref.shape[0] - chunks * stride
    part_ref[pl.ds(chunks * stride, left), :] = jnp.zeros((left, 128), BF)


def weight_kernel(x_ref, g_ref, pre_ref, act_ref, first_ref, second_ref):
    first_ref[...] = tn(x_ref[...], pre_ref[...]).astype(BF)
    second_ref[...] = tn(act_ref[...], g_ref[...]).astype(BF)


def return_kernel(rows, shift_ref, sum_ref, msg_ref, hold_ref):
    depth = hold_ref.shape[0]
    given = sum_ref.shape[0]
    base = given // 16 * 16
    hold_ref[pl.ds(base, depth - base), :] = jnp.zeros((depth - base, 128), BF)
    hold_ref[pl.ds(0, given), :] = sum_ref[...]
    shift = shift_ref[0]
    held = hold_ref[...]
    block = 256
    for b in range(msg_ref.shape[0] // block):
        row = iota((block, depth), 0) + b * block
        source = lax.shift_right_logical(row, 4)
        r = row & 15
        want = jnp.where(r < 6, source * 6 + r, rows + source * 6 + r - 6)
        want = jnp.where(r < 12, want, jnp.where(r == 12, 2 * rows, -depth)) + shift
        msg_ref[pl.ds(b * block, block), :] = jnp.dot(
            one(want == iota((block, depth), 1)), held, preferred_element_type=F32
        ).astype(BF)


def collect_kernel(code_ref, msg_ref, out_ref, rest_ref):
    held = msg_ref[...]
    depth = held.shape[0]
    tok_rows = code_ref.shape[1]
    picked = None
    for m in range(2):
        code = to_column(code_ref[m : m + 1, :])
        want = (lax.shift_right_logical(code, 3) * 2 + m) * 16 + (code & 7)
        lane = iota((tok_rows, depth), 1)
        out_ref[pl.ds(m * tok_rows, tok_rows), :] = jnp.dot(
            one(lane == want), held, preferred_element_type=F32
        ).astype(BF)
        pick = one(lane == want + 6)
        picked = pick if picked is None else picked + pick
    rest_ref[pl.ds(0, tok_rows), :] = jnp.dot(picked, held, preferred_element_type=F32).astype(BF)
    n = depth // 16
    row = iota((n, depth), 0)
    want = ((row & (n // 2 - 1)) * 2 + jnp.where(row >= n // 2, 1, 0)) * 16 + 12
    rest_ref[pl.ds(tok_rows, n), :] = jnp.dot(
        one(iota((n, depth), 1) == want), held, preferred_element_type=F32
    ).astype(BF)


def final_kernel(out_ref, rest_ref, moe_ref, token_ref, router_ref):
    tok_rows = token_ref.shape[0]
    for c in range(token_ref.shape[1] // 128):
        lanes = slice(c * 128, (c + 1) * 128)
        moe_ref[:, lanes] = out_ref[c]
        token_ref[:, lanes] = rest_ref[c, 0:tok_rows, :].astype(F32)
        router_ref[:, lanes] = rest_ref[c, tok_rows:, :].astype(F32)


def call(kernel, out, n_in, name, flops, size, scratch=(), smem_first=False):
    specs = [SM if smem_first and k == 0 else VM for k in range(n_in)]
    return pl.pallas_call(
        kernel,
        out_shape=[jax.ShapeDtypeStruct(s, d) for s, d in out],
        in_specs=specs,
        out_specs=[VM] * len(out),
        scratch_shapes=list(scratch),
        compiler_params=pltpu.CompilerParams(vmem_limit_bytes=LIMIT),
        cost_estimate=pl.CostEstimate(flops=flops, bytes_accessed=size, transcendentals=0),
        name=name,
    )


def shards(tokens, route_ids, router, w_in, w_out, out_grad):
    members, tok_rows = route_ids.shape[0], route_ids.shape[1]
    experts, width = router.shape[2], router.shape[1]
    hidden = w_in.shape[3]
    places = experts * members
    capacity = 3 * tok_rows // (2 * experts)
    rows = places * capacity
    half = width // 2
    plane = ("dp", "member")
    z_count = lax.axis_size("expert")
    z = lax.axis_index("expert")

    msg, codes = call(
        dispatch_kernel,
        [((rows * 4, half), BF), ((members, tok_rows), jnp.int32)],
        3, "dispatch", 3 << 30, 4 << 20,
    )(route_ids[:, :, 0], tokens, out_grad)
    arrived = lax.all_to_all(
        msg.reshape(places, 4 * capacity, half), plane, split_axis=0, concat_axis=0, tiled=True
    ).reshape(rows * 4, half)
    column = lax.dynamic_slice(
        router, (lax.axis_index("member"), 0, lax.axis_index("dp")), (1, width, 1)
    ).reshape(1, width)
    stride = 2 * rows + 16
    share = stride - 1
    part, x_rows, g_rows, pre_grad, scaled_act = call(
        functools.partial(expert_kernel, stride),
        [
            ((z_count * share, 128), BF),
            ((rows, width), BF),
            ((rows, width), BF),
            ((rows, hidden), BF),
            ((rows, hidden), BF),
        ],
        4, "expert", 3 << 30, 12 << 20,
    )(arrived, w_in[0, 0], w_out[0, 0], column)
    total = lax.psum_scatter(part, "expert", scatter_dimension=0, tiled=True)
    (back,) = call(
        functools.partial(return_kernel, rows),
        [((places * 16, 128), BF)],
        2, "to_tokens", 1 << 28, 1 << 20,
        scratch=[pltpu.VMEM((-(-share // 128) * 128, 128), BF)],
        smem_first=True,
    )(z.reshape(1), total)
    home = lax.all_to_all(
        back.reshape(places, 16, 128), plane, split_axis=0, concat_axis=0, tiled=True
    ).reshape(places * 16, 128)
    grad_first, grad_second = call(
        weight_kernel,
        [((width, hidden), BF), ((hidden, width), BF)],
        4, "weights", 1 << 30, 6 << 20,
    )(x_rows, g_rows, pre_grad, scaled_act)
    out_own, rest_own = call(
        collect_kernel,
        [((members * tok_rows, 128), BF), ((tok_rows + places, 128), BF)],
        2, "collect", 1 << 28, 1 << 20,
    )(codes, home)
    out_all = lax.all_gather(out_own, "expert")
    rest_all = lax.all_gather(rest_own, "expert")
    moe, token_grad, router_rows = call(
        final_kernel,
        [((members * tok_rows, width), BF), ((tok_rows, width), F32), ((places, width), F32)],
        2, "final", 1 << 20, 4 << 20,
    )(out_all, rest_all)
    router_grad = jnp.transpose(router_rows.reshape(members, experts, width), (0, 2, 1))
    return (
        moe.reshape(members, tok_rows, width),
        token_grad,
        grad_first[None, None],
        grad_second[None, None],
        router_grad,
    )


def solution(mesh):
    in_specs = (
        P(("dp", "member"), None),
        P(None, ("dp", "member"), None),
        P(),
        P("member", "dp", None, "expert"),
        P("member", "dp", "expert", None),
        P(None, ("dp", "member"), None),
    )
    out_specs = (
        P(None, ("dp", "member"), None),
        P(("dp", "member"), None),
        P("member", "dp", None, "expert"),
        P("member", "dp", "expert", None),
        P(),
    )
    return jax.shard_map(shards, mesh=mesh, in_specs=in_specs, out_specs=out_specs, check_vma=False)
```

```python
import functools

import jax
import jax.numpy as jnp
from jax import lax
from jax.experimental import pallas as pl
from jax.experimental.pallas import tpu as pltpu
from jax.sharding import PartitionSpec as P

BF = jnp.bfloat16
F32 = jnp.float32
tanh_scale = 0.7978845608028654
cubic_term = 0.044715
LIMIT = 44 << 20
FULL = 60 << 20
MOST = 52 << 20
LESS = 24 << 20
PARTS = 3
VM = pl.BlockSpec(memory_space=pltpu.VMEM)
HB = pl.BlockSpec(memory_space=pltpu.HBM)
SM = pl.BlockSpec(memory_space=pltpu.SMEM)


def iota(shape, axis):
    return lax.broadcasted_iota(jnp.int32, shape, axis)


def one(mask):
    return jnp.where(mask, 1.0, 0.0).astype(BF)


def to_column(row):
    n = row.shape[1]
    eye = iota((n, n), 0) == iota((n, n), 1)
    return jnp.sum(jnp.where(eye, row, 0), axis=1, keepdims=True)


def dispatch_kernel(
    part_ref, ids_hbm, tok_hbm, grad_hbm, msg_hbm, code_ref, ids_ref, tok_ref, grad_ref, msg_ref, sem, out_sem
):
    loads = [
        pltpu.make_async_copy(src, dst, sem.at[k])
        for k, (src, dst) in enumerate(
            ((ids_hbm, ids_ref), (tok_hbm, tok_ref), (grad_hbm, grad_ref))
        )
    ]
    for load in loads:
        load.start()
    tok_rows, width = tok_ref.shape
    half = width // 2
    loads[0].wait()
    codes = []
    for m in range(2):
        ids = ids_ref[m : m + 1, :]
        same = to_column(ids) == ids
        earlier = iota((tok_rows, tok_rows), 0) < iota((tok_rows, tok_rows), 1)
        slot = jnp.sum(jnp.where(same & earlier, 1, 0), axis=0, keepdims=True)
        code = ids * 8 + slot
        code_ref[m : m + 1, :] = code
        codes.append(code)
    loads[1].wait()
    loads[2].wait()
    sides = [
        jnp.concatenate([v[:, :half], v[:, half:]], axis=0)
        for v in (tok_ref[...], grad_ref[0], grad_ref[1])
    ]
    block = 256
    stores = []
    for b in range(msg_ref.shape[0] // block):
        row = iota((block, tok_rows), 0) + b * block
        dest = lax.shift_right_logical(row, 3)
        slot = 2 * part_ref[0] + (row & 1)
        kind = lax.shift_right_logical(row & 7, 1)
        code = lax.shift_right_logical(dest, 1) * 8 + slot
        member = dest & 1
        hit0 = (code == codes[0]) & (member == 0)
        hit1 = (code == codes[1]) & (member == 1)
        hit = hit0 | hit1
        parts = (
            [hit & (kind == 0), hit & (kind == 1)],
            [hit0 & (kind == 2), hit0 & (kind == 3)],
            [hit1 & (kind == 2), hit1 & (kind == 3)],
        )
        total = None
        for pair, side in zip(parts, sides):
            pick = jnp.concatenate([one(p) for p in pair], axis=1)
            term = jnp.dot(pick, side, preferred_element_type=F32)
            total = term if total is None else total + term
        here = pl.ds(b * block, block)
        msg_ref[here, :] = total.astype(BF)
        store = pltpu.make_async_copy(msg_ref.at[here], msg_hbm.at[here], out_sem.at[b])
        store.start()
        stores.append(store)
    for store in stores:
        store.wait()


def nt(a, b):
    return lax.dot_general(a, b, (((1,), (1,)), ((), ())), preferred_element_type=F32)


def tn(a, b):
    return lax.dot_general(a, b, (((0,), (0,)), ((), ())), preferred_element_type=F32)


def sorting():
    p = iota((256, 256), 0)
    source = (
        lax.shift_right_logical(p & 63, 1) * 8 + lax.shift_right_logical(p, 6) * 2 + (p & 1)
    )
    return one(source == iota((256, 256), 1))


def unpack(sort, msg_ref, k, x_ref, g_ref):
    half = msg_ref.shape[1]
    width = 2 * half
    part = jnp.dot(sort, msg_ref[pl.ds(k * 256, 256), :], preferred_element_type=F32).astype(BF)
    here = pl.ds(k * 64, 64)
    x_ref[here, 0:half] = part[0:64]
    x_ref[here, half:width] = part[64:128]
    g_ref[here, 0:half] = part[128:192]
    g_ref[here, half:width] = part[192:256]


def fetch(sources, msg_ref, sem):
    copies = []
    for n, source in enumerate(sources):
        for k in range(2):
            index = 2 * n + k
            copies.append(
                pltpu.make_async_copy(
                    source.at[pl.ds(k * 256, 256)],
                    msg_ref.at[pl.ds(index * 256, 256)],
                    sem.at[index],
                )
            )
    return copies


def wrap(part):
    return jnp.where(part >= PARTS, part - PARTS, part)


def expert_kernel(
    stride, part_index_ref, own_hbm, up_hbm, down_hbm, first_hbm, second_hbm, router_ref, part_ref, pre_ref, act_ref,
    msg_ref, first_ref, second_ref, x_ref, g_ref, sem, weight_sem,
):
    loads = fetch((own_hbm, up_hbm, down_hbm), msg_ref, sem)
    weights = [
        pltpu.make_async_copy(first_hbm, first_ref, weight_sem.at[0]),
        pltpu.make_async_copy(second_hbm, second_ref, weight_sem.at[1]),
    ]
    for copy in loads[:2] + weights + loads[2:]:
        copy.start()
    rows, width = x_ref.shape
    chunks = width // 128
    router = router_ref[...]
    sort = sorting()
    router_sum = jnp.zeros((1, width), F32)
    block = 128
    left = part_ref.shape[0] - chunks * stride
    part_ref[pl.ds(chunks * stride, left), :] = jnp.zeros((left, 128), BF)
    for b in range(rows // block):
        for k in range(2 * b, 2 * b + 2):
            loads[k].wait()
            unpack(sort, msg_ref, k, x_ref, g_ref)
        if b == 0:
            for copy in weights:
                copy.wait()
            first = first_ref[...]
            second = second_ref[...]
        here = pl.ds(b * block, block)
        x = x_ref[here, :]
        g = g_ref[here, :]
        xf = x.astype(F32)
        logit = jnp.sum(xf * router, axis=1, keepdims=True)
        gate = 1.0 / (1.0 + jnp.exp(-logit))
        pre = jnp.dot(x, first, preferred_element_type=F32)
        hidden = nt(g, second)
        tanh_value = jnp.tanh(tanh_scale * (pre + cubic_term * pre * pre * pre))
        act = 0.5 * pre * (1.0 + tanh_value)
        slope = 0.5 * (1.0 + tanh_value) + 0.5 * pre * (
            1.0 - tanh_value * tanh_value
        ) * tanh_scale * (1.0 + 3.0 * cubic_term * pre * pre)
        gate_grad = jnp.sum(act * hidden, axis=1, keepdims=True)
        logit_grad = gate_grad * gate * (1.0 - gate)
        pre_grad = (hidden * gate * slope).astype(BF)
        scaled_act = (act * gate).astype(BF)
        pre_ref[here, :] = pre_grad
        act_ref[here, :] = scaled_act
        router_sum = router_sum + jnp.sum(xf * logit_grad, axis=0, keepdims=True)
        place = wrap(part_index_ref[0] + (0, 2, 1)[b]) * block
        out = jnp.dot(scaled_act, second, preferred_element_type=F32).astype(BF)
        dx = (nt(pre_grad, first) + logit_grad * router).astype(BF)
        for c in range(chunks):
            lanes = slice(c * 128, (c + 1) * 128)
            at_out = pl.multiple_of(place + c * stride, 16)
            at_dx = pl.multiple_of(place + c * stride + rows, 16)
            part_ref[pl.ds(at_out, block), :] = out[:, lanes]
            part_ref[pl.ds(at_dx, block), :] = dx[:, lanes]
    for c in range(chunks):
        lanes = slice(c * 128, (c + 1) * 128)
        tail = jnp.where(iota((16, 128), 0) == 0, router_sum[:, lanes], 0.0)
        part_ref[pl.ds(c * stride + 2 * rows, 16), :] = tail.astype(BF)


def weight_kernel(
    own_hbm, up_hbm, down_hbm, pre_ref, act_ref, first_ref, second_ref, msg_ref, x_ref, g_ref, sem
):
    loads = fetch((own_hbm, up_hbm, down_hbm), msg_ref, sem)
    for load in loads:
        load.start()
    sort = sorting()
    for k, load in enumerate(loads):
        load.wait()
        unpack(sort, msg_ref, k, x_ref, g_ref)
    first_ref[...] = tn(x_ref[...], pre_ref[...]).astype(BF)
    second_ref[...] = tn(act_ref[...], g_ref[...]).astype(BF)


def return_kernel(rows, shift_ref, sum_ref, msg_ref, hold_ref):
    depth = hold_ref.shape[0]
    given = sum_ref.shape[0]
    base = given // 16 * 16
    hold_ref[pl.ds(base, depth - base), :] = jnp.zeros((depth - base, 128), BF)
    hold_ref[pl.ds(0, given), :] = sum_ref[...]
    shift = shift_ref[0]
    held = hold_ref[...]
    block = 256
    for b in range(msg_ref.shape[0] // block):
        row = iota((block, depth), 0) + b * block
        source = lax.shift_right_logical(row, 4)
        r = row & 15
        slot = jnp.where(r < 6, r, r - 6)
        want = lax.shift_right_logical(slot, 1) * (rows // PARTS) + source * 2 + (slot & 1)
        want = jnp.where(r < 6, want, rows + want)
        want = jnp.where(r < 12, want, jnp.where(r == 12, 2 * rows, -depth)) + shift
        msg_ref[pl.ds(b * block, block), :] = jnp.dot(
            one(want == iota((block, depth), 1)), held, preferred_element_type=F32
        ).astype(BF)


def collect_kernel(code_ref, msg_ref, out_ref):
    held = msg_ref[...]
    depth = held.shape[0]
    tok_rows = code_ref.shape[1]
    picked = None
    for m in range(2):
        code = to_column(code_ref[m : m + 1, :])
        want = (lax.shift_right_logical(code, 3) * 2 + m) * 16 + (code & 7)
        lane = iota((tok_rows, depth), 1)
        out_ref[pl.ds(m * tok_rows, tok_rows), :] = jnp.dot(
            one(lane == want), held, preferred_element_type=F32
        ).astype(BF)
        pick = one(lane == want + 6)
        picked = pick if picked is None else picked + pick
    out_ref[pl.ds(2 * tok_rows, tok_rows), :] = jnp.dot(picked, held, preferred_element_type=F32).astype(BF)
    n = depth // 16
    row = iota((n, depth), 0)
    want = ((row & (n // 2 - 1)) * 2 + jnp.where(row >= n // 2, 1, 0)) * 16 + 12
    out_ref[pl.ds(3 * tok_rows, n), :] = jnp.dot(
        one(iota((n, depth), 1) == want), held, preferred_element_type=F32
    ).astype(BF)


def final_kernel(part_ref, own_ref, up_ref, down_ref, moe_ref, token_ref, router_ref):
    tok_rows, width = token_ref.shape
    for ref, shift in ((own_ref, 0), (up_ref, 2), (down_ref, 1)):
        part = wrap(part_ref[0] + shift)
        for k in range(ref.shape[0]):

            @pl.when(part + PARTS * k < width // 128)
            def _():
                lanes = pl.ds(pl.multiple_of((part + PARTS * k) * 128, 128), 128)
                moe_ref[:, lanes] = ref[k, 0 : 2 * tok_rows, :]
                token_ref[:, lanes] = ref[k, 2 * tok_rows : 3 * tok_rows, :].astype(F32)
                router_ref[:, lanes] = ref[k, 3 * tok_rows :, :].astype(F32)


def call(kernel, out, specs, name, flops, size, scratch=(), out_specs=None, limit=FULL):
    return pl.pallas_call(
        kernel,
        out_shape=[jax.ShapeDtypeStruct(s, d) for s, d in out],
        in_specs=specs,
        out_specs=out_specs or [VM] * len(out),
        scratch_shapes=list(scratch),
        compiler_params=pltpu.CompilerParams(vmem_limit_bytes=limit),
        cost_estimate=pl.CostEstimate(flops=flops, bytes_accessed=size, transcendentals=0),
        name=name,
    )


def shards(tokens, route_ids, router, w_in, w_out, out_grad):
    members, tok_rows = route_ids.shape[0], route_ids.shape[1]
    experts, width = router.shape[2], router.shape[1]
    hidden = w_in.shape[3]
    places = experts * members
    capacity = 3 * tok_rows // (2 * experts)
    rows = places * capacity
    half = width // 2
    plane = ("dp", "member")
    z_count = lax.axis_size("expert")
    z = lax.axis_index("expert")
    part_index = (z % PARTS).reshape(1)
    ahead = [(k, (k + 1) % z_count) for k in range(z_count)]
    behind = [(k, (k - 1) % z_count) for k in range(z_count)]
    lines = [list(range(k, z_count, PARTS)) for k in range(PARTS)]

    dma = pltpu.SemaphoreType.DMA
    count = rows * 4 // 256
    msg, codes = call(
        dispatch_kernel,
        [((places * 8, half), BF), ((members, tok_rows), jnp.int32)],
        [SM] + [HB] * 3, "dispatch", 3 << 30, 4 << 20,
        scratch=[
            pltpu.VMEM((members, tok_rows), jnp.int32),
            pltpu.VMEM((tok_rows, width), BF),
            pltpu.VMEM((members, tok_rows, width), BF),
            pltpu.VMEM((places * 8, half), BF),
            dma((3,)),
            dma((places * 8 // 256,)),
        ],
        out_specs=[HB, VM],
    )(part_index, route_ids[:, :, 0], tokens, out_grad)
    own = lax.all_to_all(
        msg.reshape(places, 8, half), plane, split_axis=0, concat_axis=0, tiled=True
    ).reshape(places * 8, half)
    arrived = (own, lax.ppermute(own, "expert", ahead), lax.ppermute(own, "expert", behind))
    column = lax.dynamic_slice(
        router, (lax.axis_index("member"), 0, lax.axis_index("dp")), (1, width, 1)
    ).reshape(1, width)
    stride = 2 * rows + 16
    share = stride - 1
    sides = [pltpu.VMEM((rows * 4, half), BF)]
    pair = [pltpu.VMEM((rows, width), BF)] * 2
    part, pre_grad, scaled_act = call(
        functools.partial(expert_kernel, stride),
        [((z_count * share, 128), BF), ((rows, hidden), BF), ((rows, hidden), BF)],
        [SM] + [HB] * 5 + [VM], "expert", 3 << 30, 8 << 20, limit=MOST,
        scratch=sides
        + [pltpu.VMEM((width, hidden), BF), pltpu.VMEM((hidden, width), BF)]
        + pair
        + [dma((count,)), dma((2,))],
    )(part_index, *arrived, w_in[0, 0], w_out[0, 0], column)
    total = lax.psum_scatter(part, "expert", scatter_dimension=0, tiled=True)
    (back,) = call(
        functools.partial(return_kernel, rows),
        [((places * 16, 128), BF)],
        [SM, VM], "to_tokens", 1 << 28, 1 << 20,
        scratch=[pltpu.VMEM((-(-share // 128) * 128, 128), BF)],
        limit=LIMIT,
    )(z.reshape(1), total)
    home = lax.all_to_all(
        back.reshape(places, 16, 128), plane, split_axis=0, concat_axis=0, tiled=True
    ).reshape(places * 16, 128)
    grad_first, grad_second = call(
        weight_kernel,
        [((width, hidden), BF), ((hidden, width), BF)],
        [HB] * 3 + [VM] * 2, "weights", 1 << 30, 6 << 20, limit=LESS,
        scratch=sides + pair + [dma((count,))],
    )(*arrived, pre_grad, scaled_act)
    (compact,) = call(
        collect_kernel,
        [(((members + 1) * tok_rows + places, 128), BF)],
        [VM] * 2, "collect", 1 << 28, 1 << 20, limit=LIMIT,
    )(codes, home)
    line = lax.all_gather(compact, "expert", axis_index_groups=lines)
    moe, token_grad, router_rows = call(
        final_kernel,
        [((members * tok_rows, width), BF), ((tok_rows, width), F32), ((places, width), F32)],
        [SM] + [VM] * 3, "final", 1 << 20, 4 << 20, limit=LIMIT,
    )(
        part_index,
        line,
        lax.ppermute(line, "expert", ahead),
        lax.ppermute(line, "expert", behind),
    )
    router_grad = jnp.transpose(router_rows.reshape(members, experts, width), (0, 2, 1))
    return (
        moe.reshape(members, tok_rows, width),
        token_grad,
        grad_first[None, None],
        grad_second[None, None],
        router_grad,
    )


def solution(mesh):
    in_specs = (
        P(("dp", "member"), None),
        P(None, ("dp", "member"), None),
        P(),
        P("member", "dp", None, "expert"),
        P("member", "dp", "expert", None),
        P(None, ("dp", "member"), None),
    )
    out_specs = (
        P(None, ("dp", "member"), None),
        P(("dp", "member"), None),
        P("member", "dp", None, "expert"),
        P("member", "dp", "expert", None),
        P(),
    )
    return jax.shard_map(shards, mesh=mesh, in_specs=in_specs, out_specs=out_specs, check_vma=False)
```

```python
import functools

import jax
import jax.numpy as jnp
from jax import lax
from jax.experimental import pallas as pl
from jax.experimental.pallas import tpu as pltpu
from jax.sharding import PartitionSpec as P

BF = jnp.bfloat16
F32 = jnp.float32
tanh_scale = 0.7978845608028654
cubic_term = 0.044715
LIMIT = 44 << 20
FULL = 60 << 20
MOST = 52 << 20
LESS = 24 << 20
PARTS = 3
VM = pl.BlockSpec(memory_space=pltpu.VMEM)
HB = pl.BlockSpec(memory_space=pltpu.HBM)
SM = pl.BlockSpec(memory_space=pltpu.SMEM)


def iota(shape, axis):
    return lax.broadcasted_iota(jnp.int32, shape, axis)


def one(mask):
    return jnp.where(mask, 1.0, 0.0).astype(BF)


def to_column(row):
    n = row.shape[1]
    eye = iota((n, n), 0) == iota((n, n), 1)
    return jnp.sum(jnp.where(eye, row, 0), axis=1, keepdims=True)


def dispatch_kernel(
    part_ref, ids_hbm, tok_hbm, grad_hbm, msg_hbm, code_ref, ids_ref, tok_ref, grad_ref, msg_ref, sem, out_sem
):
    loads = [
        pltpu.make_async_copy(src, dst, sem.at[k])
        for k, (src, dst) in enumerate(
            ((ids_hbm, ids_ref), (tok_hbm, tok_ref), (grad_hbm, grad_ref))
        )
    ]
    for load in loads:
        load.start()
    tok_rows, width = tok_ref.shape
    half = width // 2
    loads[0].wait()
    codes = []
    for m in range(2):
        ids = ids_ref[m : m + 1, :]
        same = to_column(ids) == ids
        earlier = iota((tok_rows, tok_rows), 0) < iota((tok_rows, tok_rows), 1)
        slot = jnp.sum(jnp.where(same & earlier, 1, 0), axis=0, keepdims=True)
        code = ids * 8 + slot
        code_ref[m : m + 1, :] = code
        codes.append(code)
    loads[1].wait()
    loads[2].wait()
    sides = [
        jnp.concatenate([v[:, :half], v[:, half:]], axis=0)
        for v in (tok_ref[...], grad_ref[0], grad_ref[1])
    ]
    block = 256
    stores = []
    for b in range(msg_ref.shape[0] // block):
        row = iota((block, tok_rows), 0) + b * block
        dest = lax.shift_right_logical(row, 3)
        slot = 2 * part_ref[0] + (row & 1)
        kind = lax.shift_right_logical(row & 7, 1)
        code = lax.shift_right_logical(dest, 1) * 8 + slot
        member = dest & 1
        hit0 = (code == codes[0]) & (member == 0)
        hit1 = (code == codes[1]) & (member == 1)
        hit = hit0 | hit1
        parts = (
            [hit & (kind == 0), hit & (kind == 1)],
            [hit0 & (kind == 2), hit0 & (kind == 3)],
            [hit1 & (kind == 2), hit1 & (kind == 3)],
        )
        total = None
        for pair, side in zip(parts, sides):
            pick = jnp.concatenate([one(p) for p in pair], axis=1)
            term = jnp.dot(pick, side, preferred_element_type=F32)
            total = term if total is None else total + term
        here = pl.ds(b * block, block)
        msg_ref[here, :] = total.astype(BF)
        store = pltpu.make_async_copy(msg_ref.at[here], msg_hbm.at[here], out_sem.at[b])
        store.start()
        stores.append(store)
    for store in stores:
        store.wait()


def nt(a, b):
    return lax.dot_general(a, b, (((1,), (1,)), ((), ())), preferred_element_type=F32)


def tn(a, b):
    return lax.dot_general(a, b, (((0,), (0,)), ((), ())), preferred_element_type=F32)


def sorting():
    p = iota((256, 256), 0)
    source = (
        lax.shift_right_logical(p & 63, 1) * 8 + lax.shift_right_logical(p, 6) * 2 + (p & 1)
    )
    return one(source == iota((256, 256), 1))


def unpack(sort, msg_ref, k, x_ref, g_ref):
    half = msg_ref.shape[1]
    width = 2 * half
    part = jnp.dot(sort, msg_ref[pl.ds(k * 256, 256), :], preferred_element_type=F32).astype(BF)
    here = pl.ds(k * 64, 64)
    x_ref[here, 0:half] = part[0:64]
    x_ref[here, half:width] = part[64:128]
    g_ref[here, 0:half] = part[128:192]
    g_ref[here, half:width] = part[192:256]


def fetch(sources, msg_ref, sem):
    copies = []
    for n, source in enumerate(sources):
        for k in range(2):
            index = 2 * n + k
            copies.append(
                pltpu.make_async_copy(
                    source.at[pl.ds(k * 256, 256)],
                    msg_ref.at[pl.ds(index * 256, 256)],
                    sem.at[index],
                )
            )
    return copies


def wrap(part):
    return jnp.where(part >= PARTS, part - PARTS, part)


def expert_rows(x, g, first, second, router):
    xf = x.astype(F32)
    logit = jnp.sum(xf * router, axis=1, keepdims=True)
    gate = 1.0 / (1.0 + jnp.exp(-logit))
    pre = jnp.dot(x, first, preferred_element_type=F32)
    hidden = nt(g, second)
    tanh_value = jnp.tanh(tanh_scale * (pre + cubic_term * pre * pre * pre))
    act = 0.5 * pre * (1.0 + tanh_value)
    slope = 0.5 * (1.0 + tanh_value) + 0.5 * pre * (
        1.0 - tanh_value * tanh_value
    ) * tanh_scale * (1.0 + 3.0 * cubic_term * pre * pre)
    gate_grad = jnp.sum(act * hidden, axis=1, keepdims=True)
    logit_grad = gate_grad * gate * (1.0 - gate)
    pre_grad = (hidden * gate * slope).astype(BF)
    scaled_act = (act * gate).astype(BF)
    router_sum = jnp.sum(xf * logit_grad, axis=0, keepdims=True)
    out = jnp.dot(scaled_act, second, preferred_element_type=F32).astype(BF)
    dx = (nt(pre_grad, first) + logit_grad * router).astype(BF)
    return pre_grad, scaled_act, router_sum, out, dx


def expert_kernel(blocks, rows, stride, last, *refs):
    n = len(blocks)
    index_ref, *messages = refs[: n + 1]
    refs = refs[n + 1 :]
    if last:
        first_hbm, second_hbm, router_ref, before_ref, _, part_hbm, pre_ref, act_ref = refs[:8]
        refs = refs[8:]
    else:
        first_hbm, second_hbm, router_ref, part_hbm, pre_ref, act_ref, sum_ref = refs[:7]
        refs = refs[7:]
    msg_ref, first_ref, second_ref, x_ref, g_ref, stage_ref, rest_ref = refs[:7]
    sem, weight_sem, out_sem, rest_sem = refs[7:]
    width = x_ref.shape[1]
    chunks = width // 128
    block = rows // PARTS
    loads = fetch(messages, msg_ref, sem)
    weights = [
        pltpu.make_async_copy(first_hbm, first_ref, weight_sem.at[0]),
        pltpu.make_async_copy(second_hbm, second_ref, weight_sem.at[1]),
    ]
    for copy in loads[:2] + weights + loads[2:]:
        copy.start()
    stores = []
    if not last:
        rest_ref[...] = jnp.zeros(rest_ref.shape, BF)
        here = pl.ds(chunks * stride, rest_ref.shape[0])
        stores.append(pltpu.make_async_copy(rest_ref, part_hbm.at[here], rest_sem.at[0]))
        stores[-1].start()
    router = router_ref[...]
    sort = sorting()
    router_sum = before_ref[...] if last else jnp.zeros((1, width), F32)
    for b, shift in enumerate(blocks):
        for k in range(2 * b, 2 * b + 2):
            loads[k].wait()
            unpack(sort, msg_ref, k, x_ref, g_ref)
        if b == 0:
            for copy in weights:
                copy.wait()
            first = first_ref[...]
            second = second_ref[...]
        here = pl.ds(b * block, block)
        pre_grad, scaled_act, extra, out, dx = expert_rows(
            x_ref[here, :], g_ref[here, :], first, second, router
        )
        pre_ref[here, :] = pre_grad
        act_ref[here, :] = scaled_act
        router_sum = router_sum + extra
        place = wrap(index_ref[0] + shift) * block
        for c in range(chunks):
            lanes = slice(c * 128, (c + 1) * 128)
            for k, value in enumerate((out, dx)):
                at = (b * chunks + c) * 2 + k
                staged = pl.ds(at * block, block)
                stage_ref[staged, :] = value[:, lanes]
                there = pl.ds(pl.multiple_of(place + c * stride + k * rows, 8), block)
                stores.append(
                    pltpu.make_async_copy(
                        stage_ref.at[staged], part_hbm.at[there], out_sem.at[at]
                    )
                )
                stores[-1].start()
    if last:
        tail = stride - 2 * rows
        for c in range(chunks):
            lanes = slice(c * 128, (c + 1) * 128)
            staged = pl.ds(c * tail, tail)
            row = jnp.where(iota((tail, 128), 0) == 0, router_sum[:, lanes], 0.0)
            rest_ref[staged, :] = row.astype(BF)
            stores.append(
                pltpu.make_async_copy(
                    rest_ref.at[staged],
                    part_hbm.at[pl.ds(c * stride + 2 * rows, tail)],
                    rest_sem.at[c],
                )
            )
            stores[-1].start()
    else:
        sum_ref[...] = router_sum
    for store in stores:
        store.wait()


def weight_kernel(
    own_hbm, up_hbm, down_hbm, pre_own, act_own, pre_rest, act_rest,
    first_ref, second_ref, msg_ref, x_ref, g_ref, sem,
):
    loads = fetch((own_hbm, up_hbm, down_hbm), msg_ref, sem)
    for load in loads:
        load.start()
    sort = sorting()
    for k, load in enumerate(loads):
        load.wait()
        unpack(sort, msg_ref, k, x_ref, g_ref)
    pre_grad = jnp.concatenate([pre_own[...], pre_rest[...]], axis=0)
    scaled_act = jnp.concatenate([act_own[...], act_rest[...]], axis=0)
    first_ref[...] = tn(x_ref[...], pre_grad).astype(BF)
    second_ref[...] = tn(scaled_act, g_ref[...]).astype(BF)


def return_kernel(rows, shift_ref, sum_ref, msg_ref, hold_ref):
    depth = hold_ref.shape[0]
    given = sum_ref.shape[0]
    base = given // 16 * 16
    hold_ref[pl.ds(base, depth - base), :] = jnp.zeros((depth - base, 128), BF)
    hold_ref[pl.ds(0, given), :] = sum_ref[...]
    shift = shift_ref[0]
    held = hold_ref[...]
    block = 256
    for b in range(msg_ref.shape[0] // block):
        row = iota((block, depth), 0) + b * block
        source = lax.shift_right_logical(row, 4)
        r = row & 15
        slot = jnp.where(r < 6, r, r - 6)
        want = lax.shift_right_logical(slot, 1) * (rows // PARTS) + source * 2 + (slot & 1)
        want = jnp.where(r < 6, want, rows + want)
        want = jnp.where(r < 12, want, jnp.where(r == 12, 2 * rows, -depth)) + shift
        msg_ref[pl.ds(b * block, block), :] = jnp.dot(
            one(want == iota((block, depth), 1)), held, preferred_element_type=F32
        ).astype(BF)


def collect_kernel(code_ref, msg_ref, out_ref):
    held = msg_ref[...]
    depth = held.shape[0]
    tok_rows = code_ref.shape[1]
    picked = None
    for m in range(2):
        code = to_column(code_ref[m : m + 1, :])
        want = (lax.shift_right_logical(code, 3) * 2 + m) * 16 + (code & 7)
        lane = iota((tok_rows, depth), 1)
        out_ref[pl.ds(m * tok_rows, tok_rows), :] = jnp.dot(
            one(lane == want), held, preferred_element_type=F32
        ).astype(BF)
        pick = one(lane == want + 6)
        picked = pick if picked is None else picked + pick
    out_ref[pl.ds(2 * tok_rows, tok_rows), :] = jnp.dot(picked, held, preferred_element_type=F32).astype(BF)
    n = depth // 16
    row = iota((n, depth), 0)
    want = ((row & (n // 2 - 1)) * 2 + jnp.where(row >= n // 2, 1, 0)) * 16 + 12
    out_ref[pl.ds(3 * tok_rows, n), :] = jnp.dot(
        one(iota((n, depth), 1) == want), held, preferred_element_type=F32
    ).astype(BF)


def final_kernel(part_ref, own_ref, up_ref, down_ref, moe_ref, token_ref, router_ref):
    tok_rows, width = token_ref.shape
    for ref, shift in ((own_ref, 0), (up_ref, 2), (down_ref, 1)):
        part = wrap(part_ref[0] + shift)
        for k in range(ref.shape[0]):

            @pl.when(part + PARTS * k < width // 128)
            def _():
                lanes = pl.ds(pl.multiple_of((part + PARTS * k) * 128, 128), 128)
                moe_ref[:, lanes] = ref[k, 0 : 2 * tok_rows, :]
                token_ref[:, lanes] = ref[k, 2 * tok_rows : 3 * tok_rows, :].astype(F32)
                router_ref[:, lanes] = ref[k, 3 * tok_rows :, :].astype(F32)


def call(kernel, out, specs, name, flops, size, scratch=(), out_specs=None, limit=FULL, alias=None):
    return pl.pallas_call(
        kernel,
        out_shape=[jax.ShapeDtypeStruct(s, d) for s, d in out],
        in_specs=specs,
        out_specs=out_specs or [VM] * len(out),
        scratch_shapes=list(scratch),
        input_output_aliases=alias or {},
        compiler_params=pltpu.CompilerParams(vmem_limit_bytes=limit),
        cost_estimate=pl.CostEstimate(flops=flops, bytes_accessed=size, transcendentals=0),
        name=name,
    )


def shards(tokens, route_ids, router, w_in, w_out, out_grad):
    members, tok_rows = route_ids.shape[0], route_ids.shape[1]
    experts, width = router.shape[2], router.shape[1]
    hidden = w_in.shape[3]
    places = experts * members
    capacity = 3 * tok_rows // (2 * experts)
    rows = places * capacity
    half = width // 2
    plane = ("dp", "member")
    z_count = lax.axis_size("expert")
    z = lax.axis_index("expert")
    part_index = (z % PARTS).reshape(1)
    ahead = [(k, (k + 1) % z_count) for k in range(z_count)]
    behind = [(k, (k - 1) % z_count) for k in range(z_count)]
    lines = [list(range(k, z_count, PARTS)) for k in range(PARTS)]

    dma = pltpu.SemaphoreType.DMA
    msg, codes = call(
        dispatch_kernel,
        [((places * 8, half), BF), ((members, tok_rows), jnp.int32)],
        [SM] + [HB] * 3, "dispatch", 3 << 30, 4 << 20,
        scratch=[
            pltpu.VMEM((members, tok_rows), jnp.int32),
            pltpu.VMEM((tok_rows, width), BF),
            pltpu.VMEM((members, tok_rows, width), BF),
            pltpu.VMEM((places * 8, half), BF),
            dma((3,)),
            dma((places * 8 // 256,)),
        ],
        out_specs=[HB, VM],
    )(part_index, route_ids[:, :, 0], tokens, out_grad)
    own = lax.all_to_all(
        msg.reshape(places, 8, half), plane, split_axis=0, concat_axis=0, tiled=True
    ).reshape(places * 8, half)
    arrived = (own, lax.ppermute(own, "expert", ahead), lax.ppermute(own, "expert", behind))
    column = lax.dynamic_slice(
        router, (lax.axis_index("member"), 0, lax.axis_index("dp")), (1, width, 1)
    ).reshape(1, width)
    stride = 2 * rows + 32
    share = stride - 2
    chunks = width // 128
    block = rows // PARTS

    def expert_scratch(n, spare):
        return [
            pltpu.VMEM((n * 512, half), BF),
            pltpu.VMEM((width, hidden), BF),
            pltpu.VMEM((hidden, width), BF),
            pltpu.VMEM((n * block, width), BF),
            pltpu.VMEM((n * block, width), BF),
            pltpu.VMEM((n * chunks * 2 * block, 128), BF),
            pltpu.VMEM((spare, 128), BF),
            dma((2 * n,)),
            dma((2,)),
            dma((2 * n * chunks,)),
            dma((chunks,)),
        ]

    whole = ((z_count * share, 128), BF)
    part, pre_own, act_own, router_own = call(
        functools.partial(expert_kernel, (0,), rows, stride, False),
        [whole, ((block, hidden), BF), ((block, hidden), BF), ((1, width), F32)],
        [SM] + [HB] * 3 + [VM], "expert_own", 1 << 30, 6 << 20,
        scratch=expert_scratch(1, z_count * share - chunks * stride),
        out_specs=[HB, VM, VM, VM], limit=MOST,
    )(part_index, own, w_in[0, 0], w_out[0, 0], column)
    part, pre_rest, act_rest = call(
        functools.partial(expert_kernel, (2, 1), rows, stride, True),
        [whole, ((2 * block, hidden), BF), ((2 * block, hidden), BF)],
        [SM] + [HB] * 4 + [VM] * 2 + [HB], "expert_rest", 2 << 30, 8 << 20,
        scratch=expert_scratch(2, chunks * (stride - 2 * rows)),
        out_specs=[HB, VM, VM], limit=MOST, alias={7: 0},
    )(part_index, *arrived[1:], w_in[0, 0], w_out[0, 0], column, router_own, part)
    total = lax.psum_scatter(part, "expert", scatter_dimension=0, tiled=True)
    (back,) = call(
        functools.partial(return_kernel, rows),
        [((places * 16, 128), BF)],
        [SM, VM], "to_tokens", 1 << 28, 1 << 20,
        scratch=[pltpu.VMEM((-(-share // 128) * 128, 128), BF)],
        limit=LIMIT,
    )(2 * z.reshape(1), total)
    home = lax.all_to_all(
        back.reshape(places, 16, 128), plane, split_axis=0, concat_axis=0, tiled=True
    ).reshape(places * 16, 128)
    grad_first, grad_second = call(
        weight_kernel,
        [((width, hidden), BF), ((hidden, width), BF)],
        [HB] * 3 + [VM] * 4, "weights", 1 << 30, 6 << 20, limit=LESS,
        scratch=[pltpu.VMEM((rows * 4, half), BF)]
        + [pltpu.VMEM((rows, width), BF)] * 2
        + [dma((2 * PARTS,))],
    )(*arrived, pre_own, act_own, pre_rest, act_rest)
    (compact,) = call(
        collect_kernel,
        [(((members + 1) * tok_rows + places, 128), BF)],
        [VM] * 2, "collect", 1 << 28, 1 << 20, limit=LIMIT,
    )(codes, home)
    line = lax.all_gather(compact, "expert", axis_index_groups=lines)
    moe, token_grad, router_rows = call(
        final_kernel,
        [((members * tok_rows, width), BF), ((tok_rows, width), F32), ((places, width), F32)],
        [SM] + [VM] * 3, "final", 1 << 20, 4 << 20, limit=LIMIT,
    )(
        part_index,
        line,
        lax.ppermute(line, "expert", ahead),
        lax.ppermute(line, "expert", behind),
    )
    router_grad = jnp.transpose(router_rows.reshape(members, experts, width), (0, 2, 1))
    return (
        moe.reshape(members, tok_rows, width),
        token_grad,
        grad_first[None, None],
        grad_second[None, None],
        router_grad,
    )


def solution(mesh):
    in_specs = (
        P(("dp", "member"), None),
        P(None, ("dp", "member"), None),
        P(),
        P("member", "dp", None, "expert"),
        P("member", "dp", "expert", None),
        P(None, ("dp", "member"), None),
    )
    out_specs = (
        P(None, ("dp", "member"), None),
        P(("dp", "member"), None),
        P("member", "dp", None, "expert"),
        P("member", "dp", "expert", None),
        P(),
    )
    return jax.shard_map(shards, mesh=mesh, in_specs=in_specs, out_specs=out_specs, check_vma=False)
```

```python
import functools

import jax
import jax.numpy as jnp
from jax import lax
from jax.experimental import pallas as pl
from jax.experimental.pallas import tpu as pltpu
from jax.sharding import PartitionSpec as P

BF = jnp.bfloat16
F32 = jnp.float32
tanh_scale = 0.7978845608028654
cubic_term = 0.044715
LIMIT = 44 << 20
FULL = 60 << 20
MOST = 44 << 20
LESS = 24 << 20
PARTS = 3
VM = pl.BlockSpec(memory_space=pltpu.VMEM)
HB = pl.BlockSpec(memory_space=pltpu.HBM)
SM = pl.BlockSpec(memory_space=pltpu.SMEM)


def iota(shape, axis):
    return lax.broadcasted_iota(jnp.int32, shape, axis)


def one(mask):
    return jnp.where(mask, 1.0, 0.0).astype(BF)


def to_column(row):
    n = row.shape[1]
    eye = iota((n, n), 0) == iota((n, n), 1)
    return jnp.sum(jnp.where(eye, row, 0), axis=1, keepdims=True)


def dispatch_kernel(
    part_ref, ids_hbm, tok_hbm, grad_hbm, msg_hbm, code_ref, ids_ref, tok_ref, grad_ref, msg_ref, sem, out_sem
):
    loads = [
        pltpu.make_async_copy(src, dst, sem.at[k])
        for k, (src, dst) in enumerate(
            ((ids_hbm, ids_ref), (tok_hbm, tok_ref), (grad_hbm, grad_ref))
        )
    ]
    for load in loads:
        load.start()
    tok_rows, width = tok_ref.shape
    half = width // 2
    loads[0].wait()
    codes = []
    for m in range(2):
        ids = ids_ref[m : m + 1, :]
        same = to_column(ids) == ids
        earlier = iota((tok_rows, tok_rows), 0) < iota((tok_rows, tok_rows), 1)
        slot = jnp.sum(jnp.where(same & earlier, 1, 0), axis=0, keepdims=True)
        code = ids * 8 + slot
        code_ref[m : m + 1, :] = code
        codes.append(code)
    loads[1].wait()
    loads[2].wait()
    token = tok_ref[...]
    stores = []
    for m in range(2):
        grad = grad_ref[m]
        side = jnp.concatenate(
            [token[:, :half], token[:, half:], grad[:, :half], grad[:, half:]], axis=0
        )
        row = iota((msg_ref.shape[0] * 8, tok_rows), 0)
        kind = lax.shift_right_logical(row & 7, 1)
        code = lax.shift_right_logical(row, 3) * 8 + 2 * part_ref[0] + (row & 1)
        hit = code == codes[m]
        pick = jnp.concatenate([one(hit & (kind == k)) for k in range(4)], axis=1)
        rows = jnp.dot(pick, side, preferred_element_type=F32).astype(BF)
        msg_ref[:, m] = rows.reshape(msg_ref.shape[0], 8, half)
        stores.append(pltpu.make_async_copy(msg_ref.at[:, m], msg_hbm.at[:, m], out_sem.at[m]))
        stores[-1].start()
    for store in stores:
        store.wait()


def nt(a, b):
    return lax.dot_general(a, b, (((1,), (1,)), ((), ())), preferred_element_type=F32)


def tn(a, b):
    return lax.dot_general(a, b, (((0,), (0,)), ((), ())), preferred_element_type=F32)


def sorting():
    p = iota((256, 256), 0)
    source = (
        lax.shift_right_logical(p & 63, 1) * 8 + lax.shift_right_logical(p, 6) * 2 + (p & 1)
    )
    return one(source == iota((256, 256), 1))


def unpack(sort, msg_ref, k, x_ref, g_ref):
    half = msg_ref.shape[1]
    width = 2 * half
    part = jnp.dot(sort, msg_ref[pl.ds(k * 256, 256), :], preferred_element_type=F32).astype(BF)
    here = pl.ds(k * 64, 64)
    x_ref[here, 0:half] = part[0:64]
    x_ref[here, half:width] = part[64:128]
    g_ref[here, 0:half] = part[128:192]
    g_ref[here, half:width] = part[192:256]


def fetch(sources, msg_ref, sem):
    copies = []
    for n, source in enumerate(sources):
        for k in range(2):
            index = 2 * n + k
            copies.append(
                pltpu.make_async_copy(
                    source.at[pl.ds(k * 256, 256)],
                    msg_ref.at[pl.ds(index * 256, 256)],
                    sem.at[index],
                )
            )
    return copies


def wrap(part):
    return jnp.where(part >= PARTS, part - PARTS, part)


def expert_rows(x, g, first, second, router):
    xf = x.astype(F32)
    logit = jnp.sum(xf * router, axis=1, keepdims=True)
    gate = 1.0 / (1.0 + jnp.exp(-logit))
    pre = jnp.dot(x, first, preferred_element_type=F32)
    hidden = nt(g, second)
    tanh_value = jnp.tanh(tanh_scale * (pre + cubic_term * pre * pre * pre))
    act = 0.5 * pre * (1.0 + tanh_value)
    slope = 0.5 * (1.0 + tanh_value) + 0.5 * pre * (
        1.0 - tanh_value * tanh_value
    ) * tanh_scale * (1.0 + 3.0 * cubic_term * pre * pre)
    gate_grad = jnp.sum(act * hidden, axis=1, keepdims=True)
    logit_grad = gate_grad * gate * (1.0 - gate)
    pre_grad = (hidden * gate * slope).astype(BF)
    scaled_act = (act * gate).astype(BF)
    router_sum = jnp.sum(xf * logit_grad, axis=0, keepdims=True)
    out = jnp.dot(scaled_act, second, preferred_element_type=F32).astype(BF)
    dx = (nt(pre_grad, first) + logit_grad * router).astype(BF)
    return pre_grad, scaled_act, router_sum, out, dx


def expert_block(shift, b, stride, index_ref, msg_ref, weights, router_ref, refs):
    part_ref, kept_ref, x_ref, g_ref = refs
    rows = PARTS * x_ref.shape[0]
    block, width = x_ref.shape
    sort = sorting()
    for k in range(2):
        unpack(sort, msg_ref, k, x_ref, g_ref)
    pre_grad, scaled_act, extra, out, dx = expert_rows(
        x_ref[...], g_ref[...], *weights(), router_ref[...]
    )
    here = pl.ds(b * block, block)
    kept_ref[here, 0 : pre_grad.shape[1]] = pre_grad
    kept_ref[here, pre_grad.shape[1] :] = scaled_act
    place = wrap(index_ref[0] + shift) * block
    for c in range(width // 128):
        lanes = slice(c * 128, (c + 1) * 128)
        for k, value in enumerate((out, dx)):
            there = pl.ds(pl.multiple_of(place + c * stride + k * rows, 16), block)
            part_ref[there, :] = value[:, lanes]
    return extra


def own_kernel(
    stride, index_ref, msg_ref, first_hbm, second_hbm, router_ref,
    part_ref, kept_ref, sum_ref, first_ref, second_ref, x_ref, g_ref, sem,
):
    loads = [
        pltpu.make_async_copy(first_hbm, first_ref, sem.at[0]),
        pltpu.make_async_copy(second_hbm, second_ref, sem.at[1]),
    ]
    for load in loads:
        load.start()
    used = x_ref.shape[1] // 128 * stride
    left = part_ref.shape[0] - used
    part_ref[pl.ds(used, left), :] = jnp.zeros((left, 128), BF)

    def weights():
        for load in loads:
            load.wait()
        return first_ref[...], second_ref[...]

    sum_ref[...] = expert_block(
        0, 0, stride, index_ref, msg_ref, weights, router_ref,
        (part_ref, kept_ref, x_ref, g_ref),
    )


def rest_kernel(
    stride, index_ref, up_ref, down_ref, first_ref, second_ref, router_ref, before_ref, _,
    part_ref, kept_ref, x_ref, g_ref,
):
    rows = PARTS * x_ref.shape[1]
    router_sum = before_ref[...]
    for b, (shift, msg_ref) in enumerate(((2, up_ref), (1, down_ref))):
        router_sum = router_sum + expert_block(
            shift, b, stride, index_ref, msg_ref,
            lambda: (first_ref[...], second_ref[...]), router_ref,
            (part_ref, kept_ref, x_ref.at[b], g_ref.at[b]),
        )
    tail = stride - 2 * rows
    for c in range(x_ref.shape[2] // 128):
        lanes = slice(c * 128, (c + 1) * 128)
        row = jnp.where(iota((tail, 128), 0) == 0, router_sum[:, lanes], 0.0)
        part_ref[pl.ds(c * stride + 2 * rows, tail), :] = row.astype(BF)


def weight_kernel(
    own_hbm, up_hbm, down_hbm, own_ref, rest_ref,
    first_ref, second_ref, msg_ref, x_ref, g_ref, sem,
):
    loads = fetch((own_hbm, up_hbm, down_hbm), msg_ref, sem)
    for load in loads:
        load.start()
    sort = sorting()
    for k, load in enumerate(loads):
        load.wait()
        unpack(sort, msg_ref, k, x_ref, g_ref)
    kept = jnp.concatenate([own_ref[...], rest_ref[...]], axis=0)
    pre_grad, scaled_act = jnp.split(kept, 2, axis=1)
    first_ref[...] = tn(x_ref[...], pre_grad).astype(BF)
    second_ref[...] = tn(scaled_act, g_ref[...]).astype(BF)


def return_kernel(rows, shift_ref, sum_ref, msg_ref, hold_ref):
    depth = hold_ref.shape[0]
    given = sum_ref.shape[0]
    base = given // 16 * 16
    hold_ref[pl.ds(base, depth - base), :] = jnp.zeros((depth - base, 128), BF)
    hold_ref[pl.ds(0, given), :] = sum_ref[...]
    shift = shift_ref[0]
    held = hold_ref[...]
    block = 256
    for b in range(msg_ref.shape[0] // block):
        row = iota((block, depth), 0) + b * block
        source = lax.shift_right_logical(row, 4)
        r = row & 15
        slot = jnp.where(r < 6, r, r - 6)
        want = lax.shift_right_logical(slot, 1) * (rows // PARTS) + source * 2 + (slot & 1)
        want = jnp.where(r < 6, want, rows + want)
        want = jnp.where(r < 12, want, jnp.where(r == 12, 2 * rows, -depth)) + shift
        msg_ref[pl.ds(b * block, block), :] = jnp.dot(
            one(want == iota((block, depth), 1)), held, preferred_element_type=F32
        ).astype(BF)


def collect_kernel(code_ref, msg_ref, out_ref):
    held = msg_ref[...]
    depth = held.shape[0]
    tok_rows = code_ref.shape[1]
    picked = None
    for m in range(2):
        code = to_column(code_ref[m : m + 1, :])
        want = (lax.shift_right_logical(code, 3) * 2 + m) * 16 + (code & 7)
        lane = iota((tok_rows, depth), 1)
        out_ref[pl.ds(m * tok_rows, tok_rows), :] = jnp.dot(
            one(lane == want), held, preferred_element_type=F32
        ).astype(BF)
        pick = one(lane == want + 6)
        picked = pick if picked is None else picked + pick
    out_ref[pl.ds(2 * tok_rows, tok_rows), :] = jnp.dot(picked, held, preferred_element_type=F32).astype(BF)
    n = depth // 16
    row = iota((n, depth), 0)
    want = ((row & (n // 2 - 1)) * 2 + jnp.where(row >= n // 2, 1, 0)) * 16 + 12
    out_ref[pl.ds(3 * tok_rows, n), :] = jnp.dot(
        one(iota((n, depth), 1) == want), held, preferred_element_type=F32
    ).astype(BF)


def final_kernel(part_ref, own_ref, up_ref, down_ref, moe_ref, token_ref, router_ref):
    tok_rows, width = token_ref.shape
    for ref, shift in ((own_ref, 0), (up_ref, 2), (down_ref, 1)):
        part = wrap(part_ref[0] + shift)
        for k in range(ref.shape[0]):

            @pl.when(part + PARTS * k < width // 128)
            def _():
                lanes = pl.ds(pl.multiple_of((part + PARTS * k) * 128, 128), 128)
                moe_ref[:, lanes] = ref[k, 0 : 2 * tok_rows, :]
                token_ref[:, lanes] = ref[k, 2 * tok_rows : 3 * tok_rows, :].astype(F32)
                router_ref[:, lanes] = ref[k, 3 * tok_rows :, :].astype(F32)


def call(kernel, out, specs, name, flops, size, scratch=(), out_specs=None, limit=FULL, alias=None):
    return pl.pallas_call(
        kernel,
        out_shape=[jax.ShapeDtypeStruct(s, d) for s, d in out],
        in_specs=specs,
        out_specs=out_specs or [VM] * len(out),
        scratch_shapes=list(scratch),
        input_output_aliases=alias or {},
        compiler_params=pltpu.CompilerParams(vmem_limit_bytes=limit),
        cost_estimate=pl.CostEstimate(flops=flops, bytes_accessed=size, transcendentals=0),
        name=name,
    )


def shards(tokens, route_ids, router, w_in, w_out, out_grad):
    members, tok_rows = route_ids.shape[0], route_ids.shape[1]
    experts, width = router.shape[2], router.shape[1]
    hidden = w_in.shape[3]
    places = experts * members
    capacity = 3 * tok_rows // (2 * experts)
    rows = places * capacity
    half = width // 2
    plane = ("dp", "member")
    z_count = lax.axis_size("expert")
    z = lax.axis_index("expert")
    part_index = (z % PARTS).reshape(1)
    ahead = [(k, (k + 1) % z_count) for k in range(z_count)]
    behind = [(k, (k - 1) % z_count) for k in range(z_count)]
    lines = [list(range(k, z_count, PARTS)) for k in range(PARTS)]

    dma = pltpu.SemaphoreType.DMA
    msg, codes = call(
        dispatch_kernel,
        [((experts, members, 8, half), BF), ((members, tok_rows), jnp.int32)],
        [SM] + [HB] * 3, "dispatch", 3 << 30, 4 << 20,
        scratch=[
            pltpu.VMEM((members, tok_rows), jnp.int32),
            pltpu.VMEM((tok_rows, width), BF),
            pltpu.VMEM((members, tok_rows, width), BF),
            pltpu.VMEM((experts, members, 8, half), BF),
            dma((3,)),
            dma((2,)),
        ],
        out_specs=[HB, VM],
    )(part_index, route_ids[:, :, 0], tokens, out_grad)
    own = lax.all_to_all(
        msg.reshape(places, 8, half), plane, split_axis=0, concat_axis=0, tiled=True
    ).reshape(places * 8, half)
    arrived = (own, lax.ppermute(own, "expert", ahead), lax.ppermute(own, "expert", behind))
    column = lax.dynamic_slice(
        router, (lax.axis_index("member"), 0, lax.axis_index("dp")), (1, width, 1)
    ).reshape(1, width)
    stride = 2 * rows + 32
    share = stride - 2
    block = rows // PARTS

    whole = ((z_count * share, 128), BF)
    side = pltpu.VMEM((block, width), BF)
    part, kept_own, router_own, first, second = call(
        functools.partial(own_kernel, stride),
        [
            whole,
            ((block, 2 * hidden), BF),
            ((1, width), F32),
            ((width, hidden), BF),
            ((hidden, width), BF),
        ],
        [SM, VM, HB, HB, VM], "expert_own", 1 << 30, 6 << 20,
        scratch=[side, side, dma((2,))], limit=MOST,
    )(part_index, own, w_in[0, 0], w_out[0, 0], column)
    sides = pltpu.VMEM((2, block, width), BF)
    part, kept_rest = call(
        functools.partial(rest_kernel, stride),
        [whole, ((2 * block, 2 * hidden), BF)],
        [SM] + [VM] * 7, "expert_rest", 2 << 30, 8 << 20,
        scratch=[sides, sides], limit=MOST, alias={7: 0},
    )(part_index, *arrived[1:], first, second, column, router_own, part)
    total = lax.psum_scatter(part, "expert", scatter_dimension=0, tiled=True)
    (back,) = call(
        functools.partial(return_kernel, rows),
        [((places * 16, 128), BF)],
        [SM, VM], "to_tokens", 1 << 28, 1 << 20,
        scratch=[pltpu.VMEM((-(-share // 128) * 128, 128), BF)],
        limit=LIMIT,
    )(2 * z.reshape(1), total)
    home = lax.all_to_all(
        back.reshape(places, 16, 128), plane, split_axis=0, concat_axis=0, tiled=True
    ).reshape(places * 16, 128)
    grad_first, grad_second = call(
        weight_kernel,
        [((width, hidden), BF), ((hidden, width), BF)],
        [HB] * 3 + [VM] * 2, "weights", 1 << 30, 6 << 20, limit=LESS,
        scratch=[pltpu.VMEM((rows * 4, half), BF)]
        + [pltpu.VMEM((rows, width), BF)] * 2
        + [dma((2 * PARTS,))],
    )(*arrived, kept_own, kept_rest)
    (compact,) = call(
        collect_kernel,
        [(((members + 1) * tok_rows + places, 128), BF)],
        [VM] * 2, "collect", 1 << 28, 1 << 20, limit=LIMIT,
    )(codes, home)
    line = lax.all_gather(compact, "expert", axis_index_groups=lines)
    moe, token_grad, router_rows = call(
        final_kernel,
        [((members * tok_rows, width), BF), ((tok_rows, width), F32), ((places, width), F32)],
        [SM] + [VM] * 3, "final", 1 << 20, 4 << 20, limit=LIMIT,
    )(
        part_index,
        line,
        lax.ppermute(line, "expert", ahead),
        lax.ppermute(line, "expert", behind),
    )
    router_grad = jnp.transpose(router_rows.reshape(members, experts, width), (0, 2, 1))
    return (
        moe.reshape(members, tok_rows, width),
        token_grad,
        grad_first[None, None],
        grad_second[None, None],
        router_grad,
    )


def solution(mesh):
    in_specs = (
        P(("dp", "member"), None),
        P(None, ("dp", "member"), None),
        P(),
        P("member", "dp", None, "expert"),
        P("member", "dp", "expert", None),
        P(None, ("dp", "member"), None),
    )
    out_specs = (
        P(None, ("dp", "member"), None),
        P(("dp", "member"), None),
        P("member", "dp", None, "expert"),
        P("member", "dp", "expert", None),
        P(),
    )
    return jax.shard_map(shards, mesh=mesh, in_specs=in_specs, out_specs=out_specs, check_vma=False)
```

```python
import functools

import jax
import jax.numpy as jnp
from jax import lax
from jax.experimental import pallas as pl
from jax.experimental.pallas import tpu as pltpu
from jax.sharding import PartitionSpec as P

BF = jnp.bfloat16
F32 = jnp.float32
tanh_scale = 0.7978845608028654
cubic_term = 0.044715
LIMIT = 44 << 20
FULL = 60 << 20
MOST = 50 << 20
LESS = 24 << 20
PARTS = 3
VM = pl.BlockSpec(memory_space=pltpu.VMEM)
HB = pl.BlockSpec(memory_space=pltpu.HBM)
SM = pl.BlockSpec(memory_space=pltpu.SMEM)


def iota(shape, axis):
    return lax.broadcasted_iota(jnp.int32, shape, axis)


def one(mask):
    return jnp.where(mask, 1.0, 0.0).astype(BF)


def to_column(row):
    n = row.shape[1]
    eye = iota((n, n), 0) == iota((n, n), 1)
    return jnp.sum(jnp.where(eye, row, 0), axis=1, keepdims=True)


def dispatch_kernel(
    part_ref, ids_hbm, tok_hbm, grad_hbm, msg_hbm, code_ref, ids_ref, tok_ref, grad_ref, msg_ref, sem, out_sem
):
    loads = [
        pltpu.make_async_copy(src, dst, sem.at[k])
        for k, (src, dst) in enumerate(
            ((ids_hbm, ids_ref), (tok_hbm, tok_ref), (grad_hbm, grad_ref))
        )
    ]
    for load in loads:
        load.start()
    tok_rows, width = tok_ref.shape
    half = width // 2
    loads[0].wait()
    codes = []
    for m in range(2):
        ids = ids_ref[m : m + 1, :]
        same = to_column(ids) == ids
        earlier = iota((tok_rows, tok_rows), 0) < iota((tok_rows, tok_rows), 1)
        slot = jnp.sum(jnp.where(same & earlier, 1, 0), axis=0, keepdims=True)
        code = ids * 8 + slot
        code_ref[m : m + 1, :] = code
        codes.append(code)
    loads[1].wait()
    loads[2].wait()
    token = tok_ref[...]
    stores = []
    for m in range(2):
        grad = grad_ref[m]
        side = jnp.concatenate(
            [token[:, :half], token[:, half:], grad[:, :half], grad[:, half:]], axis=0
        )
        row = iota((msg_ref.shape[0] * 8, tok_rows), 0)
        kind = lax.shift_right_logical(row & 7, 1)
        code = lax.shift_right_logical(row, 3) * 8 + 2 * part_ref[0] + (row & 1)
        hit = code == codes[m]
        pick = jnp.concatenate([one(hit & (kind == k)) for k in range(4)], axis=1)
        rows = jnp.dot(pick, side, preferred_element_type=F32).astype(BF)
        msg_ref[:, m] = rows.reshape(msg_ref.shape[0], 8, half)
        stores.append(pltpu.make_async_copy(msg_ref.at[:, m], msg_hbm.at[:, m], out_sem.at[m]))
        stores[-1].start()
    for store in stores:
        store.wait()


def nt(a, b):
    return lax.dot_general(a, b, (((1,), (1,)), ((), ())), preferred_element_type=F32)


def tn(a, b):
    return lax.dot_general(a, b, (((0,), (0,)), ((), ())), preferred_element_type=F32)


def sorting():
    p = iota((256, 256), 0)
    source = (
        lax.shift_right_logical(p & 63, 1) * 8 + lax.shift_right_logical(p, 6) * 2 + (p & 1)
    )
    return one(source == iota((256, 256), 1))


def unpack(sort, msg_ref, k, x_ref, g_ref):
    half = msg_ref.shape[1]
    width = 2 * half
    part = jnp.dot(sort, msg_ref[pl.ds(k * 256, 256), :], preferred_element_type=F32).astype(BF)
    here = pl.ds(k * 64, 64)
    x_ref[here, 0:half] = part[0:64]
    x_ref[here, half:width] = part[64:128]
    g_ref[here, 0:half] = part[128:192]
    g_ref[here, half:width] = part[192:256]


def fetch(sources, msg_ref, sem):
    copies = []
    for n, source in enumerate(sources):
        for k in range(2):
            index = 2 * n + k
            copies.append(
                pltpu.make_async_copy(
                    source.at[pl.ds(k * 256, 256)],
                    msg_ref.at[pl.ds(index * 256, 256)],
                    sem.at[index],
                )
            )
    return copies


def wrap(part):
    return jnp.where(part >= PARTS, part - PARTS, part)


def expert_block(shift, b, stride, index_ref, msg_ref, weights, router_ref, refs, stores):
    part_hbm, kept_ref, x_ref, g_ref, stage_ref, sem = refs
    block, width = x_ref.shape
    rows = PARTS * block
    chunks = width // 128
    sort = sorting()
    for k in range(2):
        unpack(sort, msg_ref, k, x_ref, g_ref)
    x, g, router = x_ref[...], g_ref[...], router_ref[...]
    place = wrap(index_ref[0] + shift) * block

    def send(value, k):
        for c in range(chunks):
            at = (b * 2 + k) * chunks + c
            staged = pl.ds(at * block, block)
            stage_ref[staged, :] = value[:, c * 128 : (c + 1) * 128]
            there = pl.ds(pl.multiple_of(place + c * stride + k * rows, 16), block)
            stores.append(
                pltpu.make_async_copy(stage_ref.at[staged], part_hbm.at[there], sem.at[at])
            )
            stores[-1].start()

    xf = x.astype(F32)
    logit = jnp.sum(xf * router, axis=1, keepdims=True)
    gate = 1.0 / (1.0 + jnp.exp(-logit))
    first, second = weights()
    pre = jnp.dot(x, first, preferred_element_type=F32)
    hidden_grad = nt(g, second)
    tanh_value = jnp.tanh(tanh_scale * (pre + cubic_term * pre * pre * pre))
    act = 0.5 * pre * (1.0 + tanh_value)
    scaled_act = (act * gate).astype(BF)
    send(jnp.dot(scaled_act, second, preferred_element_type=F32).astype(BF), 0)
    slope = 0.5 * (1.0 + tanh_value) + 0.5 * pre * (
        1.0 - tanh_value * tanh_value
    ) * tanh_scale * (1.0 + 3.0 * cubic_term * pre * pre)
    gate_grad = jnp.sum(act * hidden_grad, axis=1, keepdims=True)
    logit_grad = gate_grad * gate * (1.0 - gate)
    pre_grad = (hidden_grad * gate * slope).astype(BF)
    send((nt(pre_grad, first) + logit_grad * router).astype(BF), 1)
    here = pl.ds(b * block, block)
    hidden = pre_grad.shape[1]
    kept_ref[here, 0:hidden] = pre_grad
    kept_ref[here, hidden:] = scaled_act
    return jnp.sum(xf * logit_grad, axis=0, keepdims=True)


def own_kernel(
    stride, index_ref, msg_ref, first_hbm, second_hbm, router_ref,
    part_hbm, kept_ref, sum_ref, first_ref, second_ref,
    x_ref, g_ref, stage_ref, zero_ref, sem, load_sem, zero_sem,
):
    loads = [
        pltpu.make_async_copy(first_hbm, first_ref, load_sem.at[0]),
        pltpu.make_async_copy(second_hbm, second_ref, load_sem.at[1]),
    ]
    for load in loads:
        load.start()
    zero_ref[...] = jnp.zeros(zero_ref.shape, BF)
    there = pl.ds(x_ref.shape[1] // 128 * stride, zero_ref.shape[0])
    stores = [pltpu.make_async_copy(zero_ref, part_hbm.at[there], zero_sem)]
    stores[0].start()

    def weights():
        for load in loads:
            load.wait()
        return first_ref[...], second_ref[...]

    sum_ref[...] = expert_block(
        0, 0, stride, index_ref, msg_ref, weights, router_ref,
        (part_hbm, kept_ref, x_ref, g_ref, stage_ref, sem), stores,
    )
    for store in stores:
        store.wait()


def rest_kernel(
    stride, index_ref, up_ref, down_ref, first_ref, second_ref, router_ref, before_ref, _,
    part_hbm, kept_ref, x_ref, g_ref, stage_ref, tail_ref, sem, tail_sem,
):
    rows = PARTS * x_ref.shape[1]
    router_sum = before_ref[...]
    stores = []
    for b, (shift, msg_ref) in enumerate(((2, up_ref), (1, down_ref))):
        router_sum = router_sum + expert_block(
            shift, b, stride, index_ref, msg_ref,
            lambda: (first_ref[...], second_ref[...]), router_ref,
            (part_hbm, kept_ref, x_ref.at[b], g_ref.at[b], stage_ref, sem), stores,
        )
    tail = stride - 2 * rows
    for c in range(x_ref.shape[2] // 128):
        lanes = slice(c * 128, (c + 1) * 128)
        row = jnp.where(iota((tail, 128), 0) == 0, router_sum[:, lanes], 0.0)
        staged = pl.ds(c * tail, tail)
        tail_ref[staged, :] = row.astype(BF)
        there = pl.ds(c * stride + 2 * rows, tail)
        stores.append(
            pltpu.make_async_copy(tail_ref.at[staged], part_hbm.at[there], tail_sem.at[c])
        )
        stores[-1].start()
    for store in stores:
        store.wait()


def weight_kernel(
    own_hbm, up_hbm, down_hbm, own_ref, rest_ref,
    first_ref, second_ref, msg_ref, x_ref, g_ref, sem,
):
    loads = fetch((own_hbm, up_hbm, down_hbm), msg_ref, sem)
    for load in loads:
        load.start()
    sort = sorting()
    for k, load in enumerate(loads):
        load.wait()
        unpack(sort, msg_ref, k, x_ref, g_ref)
    kept = jnp.concatenate([own_ref[...], rest_ref[...]], axis=0)
    pre_grad, scaled_act = jnp.split(kept, 2, axis=1)
    first_ref[...] = tn(x_ref[...], pre_grad).astype(BF)
    second_ref[...] = tn(scaled_act, g_ref[...]).astype(BF)


def return_kernel(rows, shift_ref, sum_ref, msg_ref, hold_ref):
    depth = hold_ref.shape[0]
    given = sum_ref.shape[0]
    base = given // 16 * 16
    hold_ref[pl.ds(base, depth - base), :] = jnp.zeros((depth - base, 128), BF)
    hold_ref[pl.ds(0, given), :] = sum_ref[...]
    shift = shift_ref[0]
    held = hold_ref[...]
    block = 256
    for b in range(msg_ref.shape[0] // block):
        row = iota((block, depth), 0) + b * block
        source = lax.shift_right_logical(row, 4)
        r = row & 15
        slot = jnp.where(r < 6, r, r - 6)
        want = lax.shift_right_logical(slot, 1) * (rows // PARTS) + source * 2 + (slot & 1)
        want = jnp.where(r < 6, want, rows + want)
        want = jnp.where(r < 12, want, jnp.where(r == 12, 2 * rows, -depth)) + shift
        msg_ref[pl.ds(b * block, block), :] = jnp.dot(
            one(want == iota((block, depth), 1)), held, preferred_element_type=F32
        ).astype(BF)


def collect_kernel(code_ref, msg_ref, out_ref):
    held = msg_ref[...]
    depth = held.shape[0]
    tok_rows = code_ref.shape[1]
    picked = None
    for m in range(2):
        code = to_column(code_ref[m : m + 1, :])
        want = (lax.shift_right_logical(code, 3) * 2 + m) * 16 + (code & 7)
        lane = iota((tok_rows, depth), 1)
        out_ref[pl.ds(m * tok_rows, tok_rows), :] = jnp.dot(
            one(lane == want), held, preferred_element_type=F32
        ).astype(BF)
        pick = one(lane == want + 6)
        picked = pick if picked is None else picked + pick
    out_ref[pl.ds(2 * tok_rows, tok_rows), :] = jnp.dot(picked, held, preferred_element_type=F32).astype(BF)
    n = depth // 16
    row = iota((n, depth), 0)
    want = ((row & (n // 2 - 1)) * 2 + jnp.where(row >= n // 2, 1, 0)) * 16 + 12
    out_ref[pl.ds(3 * tok_rows, n), :] = jnp.dot(
        one(iota((n, depth), 1) == want), held, preferred_element_type=F32
    ).astype(BF)


def final_kernel(part_ref, own_ref, up_ref, down_ref, moe_ref, token_ref, router_ref):
    tok_rows, width = token_ref.shape
    for ref, shift in ((own_ref, 0), (up_ref, 2), (down_ref, 1)):
        part = wrap(part_ref[0] + shift)
        for k in range(ref.shape[0]):

            @pl.when(part + PARTS * k < width // 128)
            def _():
                lanes = pl.ds(pl.multiple_of((part + PARTS * k) * 128, 128), 128)
                moe_ref[:, lanes] = ref[k, 0 : 2 * tok_rows, :]
                token_ref[:, lanes] = ref[k, 2 * tok_rows : 3 * tok_rows, :].astype(F32)
                router_ref[:, lanes] = ref[k, 3 * tok_rows :, :].astype(F32)


def call(kernel, out, specs, name, flops, size, scratch=(), out_specs=None, limit=FULL, alias=None):
    return pl.pallas_call(
        kernel,
        out_shape=[jax.ShapeDtypeStruct(s, d) for s, d in out],
        in_specs=specs,
        out_specs=out_specs or [VM] * len(out),
        scratch_shapes=list(scratch),
        input_output_aliases=alias or {},
        compiler_params=pltpu.CompilerParams(vmem_limit_bytes=limit),
        cost_estimate=pl.CostEstimate(flops=flops, bytes_accessed=size, transcendentals=0),
        name=name,
    )


def shards(tokens, route_ids, router, w_in, w_out, out_grad):
    members, tok_rows = route_ids.shape[0], route_ids.shape[1]
    experts, width = router.shape[2], router.shape[1]
    hidden = w_in.shape[3]
    places = experts * members
    capacity = 3 * tok_rows // (2 * experts)
    rows = places * capacity
    half = width // 2
    plane = ("dp", "member")
    z_count = lax.axis_size("expert")
    z = lax.axis_index("expert")
    part_index = (z % PARTS).reshape(1)
    ahead = [(k, (k + 1) % z_count) for k in range(z_count)]
    behind = [(k, (k - 1) % z_count) for k in range(z_count)]
    lines = [list(range(k, z_count, PARTS)) for k in range(PARTS)]

    dma = pltpu.SemaphoreType.DMA
    msg, codes = call(
        dispatch_kernel,
        [((experts, members, 8, half), BF), ((members, tok_rows), jnp.int32)],
        [SM] + [HB] * 3, "dispatch", 3 << 30, 4 << 20,
        scratch=[
            pltpu.VMEM((members, tok_rows), jnp.int32),
            pltpu.VMEM((tok_rows, width), BF),
            pltpu.VMEM((members, tok_rows, width), BF),
            pltpu.VMEM((experts, members, 8, half), BF),
            dma((3,)),
            dma((2,)),
        ],
        out_specs=[HB, VM],
    )(part_index, route_ids[:, :, 0], tokens, out_grad)
    own = lax.all_to_all(
        msg.reshape(places, 8, half), plane, split_axis=0, concat_axis=0, tiled=True
    ).reshape(places * 8, half)
    arrived = (own, lax.ppermute(own, "expert", ahead), lax.ppermute(own, "expert", behind))
    column = lax.dynamic_slice(
        router, (lax.axis_index("member"), 0, lax.axis_index("dp")), (1, width, 1)
    ).reshape(1, width)
    stride = 2 * rows + 32
    share = stride - 2
    block = rows // PARTS
    chunks = width // 128
    whole = ((z_count * share, 128), BF)
    side = pltpu.VMEM((block, width), BF)
    part, kept_own, router_own, first, second = call(
        functools.partial(own_kernel, stride),
        [
            whole,
            ((block, 2 * hidden), BF),
            ((1, width), F32),
            ((width, hidden), BF),
            ((hidden, width), BF),
        ],
        [SM, VM, HB, HB, VM], "expert_own", 1 << 30, 6 << 20,
        scratch=[
            side,
            side,
            pltpu.VMEM((2 * chunks * block, 128), BF),
            pltpu.VMEM((z_count * share - chunks * stride, 128), BF),
            dma((2 * chunks,)),
            dma((2,)),
            dma(()),
        ],
        out_specs=[HB] + [VM] * 4, limit=MOST,
    )(part_index, own, w_in[0, 0], w_out[0, 0], column)
    sides = pltpu.VMEM((2, block, width), BF)
    part, kept_rest = call(
        functools.partial(rest_kernel, stride),
        [whole, ((2 * block, 2 * hidden), BF)],
        [SM] + [VM] * 6 + [HB], "expert_rest", 2 << 30, 8 << 20,
        scratch=[
            sides,
            sides,
            pltpu.VMEM((4 * chunks * block, 128), BF),
            pltpu.VMEM((chunks * (stride - 2 * rows), 128), BF),
            dma((4 * chunks,)),
            dma((chunks,)),
        ],
        out_specs=[HB, VM], limit=MOST, alias={7: 0},
    )(part_index, *arrived[1:], first, second, column, router_own, part)
    total = lax.psum_scatter(part, "expert", scatter_dimension=0, tiled=True)
    (back,) = call(
        functools.partial(return_kernel, rows),
        [((places * 16, 128), BF)],
        [SM, VM], "to_tokens", 1 << 28, 1 << 20,
        scratch=[pltpu.VMEM((-(-share // 128) * 128, 128), BF)],
        limit=LIMIT,
    )(2 * z.reshape(1), total)
    home = lax.all_to_all(
        back.reshape(places, 16, 128), plane, split_axis=0, concat_axis=0, tiled=True
    ).reshape(places * 16, 128)
    grad_first, grad_second = call(
        weight_kernel,
        [((width, hidden), BF), ((hidden, width), BF)],
        [HB] * 3 + [VM] * 2, "weights", 1 << 30, 6 << 20, limit=LESS,
        scratch=[pltpu.VMEM((rows * 4, half), BF)]
        + [pltpu.VMEM((rows, width), BF)] * 2
        + [dma((2 * PARTS,))],
    )(*arrived, kept_own, kept_rest)
    (compact,) = call(
        collect_kernel,
        [(((members + 1) * tok_rows + places, 128), BF)],
        [VM] * 2, "collect", 1 << 28, 1 << 20, limit=LIMIT,
    )(codes, home)
    line = lax.all_gather(compact, "expert", axis_index_groups=lines)
    moe, token_grad, router_rows = call(
        final_kernel,
        [((members * tok_rows, width), BF), ((tok_rows, width), F32), ((places, width), F32)],
        [SM] + [VM] * 3, "final", 1 << 20, 4 << 20, limit=LIMIT,
    )(
        part_index,
        line,
        lax.ppermute(line, "expert", ahead),
        lax.ppermute(line, "expert", behind),
    )
    router_grad = jnp.transpose(router_rows.reshape(members, experts, width), (0, 2, 1))
    return (
        moe.reshape(members, tok_rows, width),
        token_grad,
        grad_first[None, None],
        grad_second[None, None],
        router_grad,
    )


def solution(mesh):
    in_specs = (
        P(("dp", "member"), None),
        P(None, ("dp", "member"), None),
        P(),
        P("member", "dp", None, "expert"),
        P("member", "dp", "expert", None),
        P(None, ("dp", "member"), None),
    )
    out_specs = (
        P(None, ("dp", "member"), None),
        P(("dp", "member"), None),
        P("member", "dp", None, "expert"),
        P("member", "dp", "expert", None),
        P(),
    )
    return jax.shard_map(shards, mesh=mesh, in_specs=in_specs, out_specs=out_specs, check_vma=False)
```

```python
import functools

import jax
import jax.numpy as jnp
from jax import lax
from jax.experimental import pallas as pl
from jax.experimental.pallas import tpu as pltpu
from jax.sharding import PartitionSpec as P

BF = jnp.bfloat16
F32 = jnp.float32
tanh_scale = 0.7978845608028654
cubic_term = 0.044715
LIMIT = 44 << 20
FULL = 60 << 20
MOST = 50 << 20
LESS = 24 << 20
PARTS = 3
VM = pl.BlockSpec(memory_space=pltpu.VMEM)
HB = pl.BlockSpec(memory_space=pltpu.HBM)
SM = pl.BlockSpec(memory_space=pltpu.SMEM)


def iota(shape, axis):
    return lax.broadcasted_iota(jnp.int32, shape, axis)


def one(mask):
    return jnp.where(mask, 1.0, 0.0).astype(BF)


def to_column(row):
    n = row.shape[1]
    eye = iota((n, n), 0) == iota((n, n), 1)
    return jnp.sum(jnp.where(eye, row, 0), axis=1, keepdims=True)


def dispatch_kernel(
    part_ref, ids_hbm, tok_hbm, grad_hbm, msg_hbm, code_ref, ids_ref, tok_ref, grad_ref, msg_ref, sem, out_sem
):
    loads = [
        pltpu.make_async_copy(src, dst, sem.at[k])
        for k, (src, dst) in enumerate(
            (
                (ids_hbm, ids_ref),
                (tok_hbm, tok_ref),
                (grad_hbm.at[0], grad_ref.at[0]),
                (grad_hbm.at[1], grad_ref.at[1]),
            )
        )
    ]
    for load in loads:
        load.start()
    tok_rows, width = tok_ref.shape
    half = width // 2
    loads[0].wait()
    codes = []
    for m in range(2):
        ids = ids_ref[m : m + 1, :]
        same = to_column(ids) == ids
        earlier = iota((tok_rows, tok_rows), 0) < iota((tok_rows, tok_rows), 1)
        slot = jnp.sum(jnp.where(same & earlier, 1, 0), axis=0, keepdims=True)
        code = ids * 8 + slot
        code_ref[m : m + 1, :] = code
        codes.append(code)
    loads[1].wait()
    token = tok_ref[...]
    stores = []
    for m in range(2):
        loads[2 + m].wait()
        grad = grad_ref[m]
        side = jnp.concatenate(
            [token[:, :half], token[:, half:], grad[:, :half], grad[:, half:]], axis=0
        )
        row = iota((msg_ref.shape[0] * 8, tok_rows), 0)
        kind = lax.shift_right_logical(row & 7, 1)
        code = lax.shift_right_logical(row, 3) * 8 + 2 * part_ref[0] + (row & 1)
        hit = code == codes[m]
        pick = jnp.concatenate([one(hit & (kind == k)) for k in range(4)], axis=1)
        rows = jnp.dot(pick, side, preferred_element_type=F32).astype(BF)
        msg_ref[:, m] = rows.reshape(msg_ref.shape[0], 8, half)
        stores.append(pltpu.make_async_copy(msg_ref.at[:, m], msg_hbm.at[:, m], out_sem.at[m]))
        stores[-1].start()
    for store in stores:
        store.wait()


def nt(a, b):
    return lax.dot_general(a, b, (((1,), (1,)), ((), ())), preferred_element_type=F32)


def tn(a, b):
    return lax.dot_general(a, b, (((0,), (0,)), ((), ())), preferred_element_type=F32)


def sorting():
    p = iota((256, 256), 0)
    source = (
        lax.shift_right_logical(p & 63, 1) * 8 + lax.shift_right_logical(p, 6) * 2 + (p & 1)
    )
    return one(source == iota((256, 256), 1))


def unpack(sort, msg_ref, k, x_ref, g_ref):
    half = msg_ref.shape[1]
    width = 2 * half
    part = jnp.dot(sort, msg_ref[pl.ds(k * 256, 256), :], preferred_element_type=F32).astype(BF)
    here = pl.ds(k * 64, 64)
    x_ref[here, 0:half] = part[0:64]
    x_ref[here, half:width] = part[64:128]
    g_ref[here, 0:half] = part[128:192]
    g_ref[here, half:width] = part[192:256]


def fetch(sources, msg_ref, sem):
    copies = []
    for n, source in enumerate(sources):
        for k in range(2):
            index = 2 * n + k
            copies.append(
                pltpu.make_async_copy(
                    source.at[pl.ds(k * 256, 256)],
                    msg_ref.at[pl.ds(index * 256, 256)],
                    sem.at[index],
                )
            )
    return copies


def wrap(part):
    return jnp.where(part >= PARTS, part - PARTS, part)


def expert_block(rows, stride, index_ref, messages, weights, router_ref, refs, stores):
    part_hbm, kept_ref, x_ref, g_ref, stage_ref, sem = refs
    block = rows // PARTS
    chunks = x_ref.shape[1] // 128
    sort = sorting()
    for n, (_, msg_ref) in enumerate(messages):
        for k in range(2):
            unpack(sort, msg_ref, k, x_ref.at[pl.ds(n * block, block)], g_ref.at[pl.ds(n * block, block)])
    x, g, router = x_ref[...], g_ref[...], router_ref[...]

    def send(value, k):
        for n, (shift, _) in enumerate(messages):
            place = wrap(index_ref[0] + shift) * block
            for c in range(chunks):
                at = (n * 2 + k) * chunks + c
                staged = pl.ds(at * block, block)
                stage_ref[staged, :] = value[
                    n * block : (n + 1) * block, c * 128 : (c + 1) * 128
                ]
                there = pl.ds(pl.multiple_of(place + c * stride + k * rows, 16), block)
                stores.append(
                    pltpu.make_async_copy(stage_ref.at[staged], part_hbm.at[there], sem.at[at])
                )
                stores[-1].start()

    xf = x.astype(F32)
    logit = jnp.sum(xf * router, axis=1, keepdims=True)
    gate = 1.0 / (1.0 + jnp.exp(-logit))
    first, second = weights()
    pre = jnp.dot(x, first, preferred_element_type=F32)
    hidden_grad = nt(g, second)
    tanh_value = jnp.tanh(tanh_scale * (pre + cubic_term * pre * pre * pre))
    act = 0.5 * pre * (1.0 + tanh_value)
    scaled_act = (act * gate).astype(BF)
    send(jnp.dot(scaled_act, second, preferred_element_type=F32).astype(BF), 0)
    slope = 0.5 * (1.0 + tanh_value) + 0.5 * pre * (
        1.0 - tanh_value * tanh_value
    ) * tanh_scale * (1.0 + 3.0 * cubic_term * pre * pre)
    gate_grad = jnp.sum(act * hidden_grad, axis=1, keepdims=True)
    logit_grad = gate_grad * gate * (1.0 - gate)
    pre_grad = (hidden_grad * gate * slope).astype(BF)
    send((nt(pre_grad, first) + logit_grad * router).astype(BF), 1)
    hidden = pre_grad.shape[1]
    kept_ref[:, 0:hidden] = pre_grad
    kept_ref[:, hidden:] = scaled_act
    return jnp.sum(xf * logit_grad, axis=0, keepdims=True)


def own_kernel(
    stride, index_ref, msg_ref, first_hbm, second_hbm, router_ref,
    part_hbm, kept_ref, sum_ref, first_ref, second_ref,
    x_ref, g_ref, stage_ref, zero_ref, sem, load_sem, zero_sem,
):
    loads = [
        pltpu.make_async_copy(first_hbm, first_ref, load_sem.at[0]),
        pltpu.make_async_copy(second_hbm, second_ref, load_sem.at[1]),
    ]
    for load in loads:
        load.start()
    zero_ref[...] = jnp.zeros(zero_ref.shape, BF)
    there = pl.ds(x_ref.shape[1] // 128 * stride, zero_ref.shape[0])
    stores = [pltpu.make_async_copy(zero_ref, part_hbm.at[there], zero_sem)]
    stores[0].start()

    def weights():
        for load in loads:
            load.wait()
        return first_ref[...], second_ref[...]

    sum_ref[...] = expert_block(
        PARTS * x_ref.shape[0], stride, index_ref, [(0, msg_ref)], weights, router_ref,
        (part_hbm, kept_ref, x_ref, g_ref, stage_ref, sem), stores,
    )
    for store in stores:
        store.wait()


def rest_kernel(
    stride, index_ref, up_ref, down_ref, first_ref, second_ref, router_ref, before_ref, _,
    part_hbm, kept_ref, x_ref, g_ref, stage_ref, tail_ref, sem, tail_sem,
):
    rows = PARTS * x_ref.shape[0] // 2
    stores = []
    router_sum = before_ref[...] + expert_block(
        rows, stride, index_ref, [(2, up_ref), (1, down_ref)],
        lambda: (first_ref[...], second_ref[...]), router_ref,
        (part_hbm, kept_ref, x_ref, g_ref, stage_ref, sem), stores,
    )
    tail = stride - 2 * rows
    for c in range(x_ref.shape[1] // 128):
        lanes = slice(c * 128, (c + 1) * 128)
        row = jnp.where(iota((tail, 128), 0) == 0, router_sum[:, lanes], 0.0)
        staged = pl.ds(c * tail, tail)
        tail_ref[staged, :] = row.astype(BF)
        there = pl.ds(c * stride + 2 * rows, tail)
        stores.append(
            pltpu.make_async_copy(tail_ref.at[staged], part_hbm.at[there], tail_sem.at[c])
        )
        stores[-1].start()
    for store in stores:
        store.wait()


def weight_kernel(
    own_hbm, up_hbm, down_hbm, own_ref, rest_ref,
    first_ref, second_ref, msg_ref, x_ref, g_ref, sem,
):
    loads = fetch((own_hbm, up_hbm, down_hbm), msg_ref, sem)
    for load in loads:
        load.start()
    sort = sorting()
    for k, load in enumerate(loads):
        load.wait()
        unpack(sort, msg_ref, k, x_ref, g_ref)
    kept = jnp.concatenate([own_ref[...], rest_ref[...]], axis=0)
    pre_grad, scaled_act = jnp.split(kept, 2, axis=1)
    first_ref[...] = tn(x_ref[...], pre_grad).astype(BF)
    second_ref[...] = tn(scaled_act, g_ref[...]).astype(BF)


def return_kernel(rows, shift_ref, sum_ref, msg_ref, hold_ref):
    depth = hold_ref.shape[0]
    given = sum_ref.shape[0]
    base = given // 16 * 16
    hold_ref[pl.ds(base, depth - base), :] = jnp.zeros((depth - base, 128), BF)
    hold_ref[pl.ds(0, given), :] = sum_ref[...]
    shift = shift_ref[0]
    held = hold_ref[...]
    block = 256
    for b in range(msg_ref.shape[0] // block):
        row = iota((block, depth), 0) + b * block
        source = lax.shift_right_logical(row, 4)
        r = row & 15
        slot = jnp.where(r < 6, r, r - 6)
        want = lax.shift_right_logical(slot, 1) * (rows // PARTS) + source * 2 + (slot & 1)
        want = jnp.where(r < 6, want, rows + want)
        want = jnp.where(r < 12, want, jnp.where(r == 12, 2 * rows, -depth)) + shift
        msg_ref[pl.ds(b * block, block), :] = jnp.dot(
            one(want == iota((block, depth), 1)), held, preferred_element_type=F32
        ).astype(BF)


def collect_kernel(code_ref, msg_ref, out_ref):
    held = msg_ref[...]
    depth = held.shape[0]
    tok_rows = code_ref.shape[1]
    picked = None
    for m in range(2):
        code = to_column(code_ref[m : m + 1, :])
        want = (lax.shift_right_logical(code, 3) * 2 + m) * 16 + (code & 7)
        lane = iota((tok_rows, depth), 1)
        out_ref[pl.ds(m * tok_rows, tok_rows), :] = jnp.dot(
            one(lane == want), held, preferred_element_type=F32
        ).astype(BF)
        pick = one(lane == want + 6)
        picked = pick if picked is None else picked + pick
    out_ref[pl.ds(2 * tok_rows, tok_rows), :] = jnp.dot(picked, held, preferred_element_type=F32).astype(BF)
    n = depth // 16
    row = iota((n, depth), 0)
    want = ((row & (n // 2 - 1)) * 2 + jnp.where(row >= n // 2, 1, 0)) * 16 + 12
    out_ref[pl.ds(3 * tok_rows, n), :] = jnp.dot(
        one(iota((n, depth), 1) == want), held, preferred_element_type=F32
    ).astype(BF)


def final_kernel(part_ref, own_ref, up_ref, down_ref, moe_ref, token_ref, router_ref):
    tok_rows, width = token_ref.shape
    for ref, shift in ((own_ref, 0), (up_ref, 2), (down_ref, 1)):
        part = wrap(part_ref[0] + shift)
        for k in range(ref.shape[0]):

            @pl.when(part + PARTS * k < width // 128)
            def _():
                lanes = pl.ds(pl.multiple_of((part + PARTS * k) * 128, 128), 128)
                moe_ref[:, lanes] = ref[k, 0 : 2 * tok_rows, :]
                token_ref[:, lanes] = ref[k, 2 * tok_rows : 3 * tok_rows, :].astype(F32)
                router_ref[:, lanes] = ref[k, 3 * tok_rows :, :].astype(F32)


def call(kernel, out, specs, name, flops, size, scratch=(), out_specs=None, limit=FULL, alias=None):
    return pl.pallas_call(
        kernel,
        out_shape=[jax.ShapeDtypeStruct(s, d) for s, d in out],
        in_specs=specs,
        out_specs=out_specs or [VM] * len(out),
        scratch_shapes=list(scratch),
        input_output_aliases=alias or {},
        compiler_params=pltpu.CompilerParams(vmem_limit_bytes=limit),
        cost_estimate=pl.CostEstimate(flops=flops, bytes_accessed=size, transcendentals=0),
        name=name,
    )


def shards(tokens, route_ids, router, w_in, w_out, out_grad):
    members, tok_rows = route_ids.shape[0], route_ids.shape[1]
    experts, width = router.shape[2], router.shape[1]
    hidden = w_in.shape[3]
    places = experts * members
    capacity = 3 * tok_rows // (2 * experts)
    rows = places * capacity
    half = width // 2
    plane = ("dp", "member")
    z_count = lax.axis_size("expert")
    z = lax.axis_index("expert")
    part_index = (z % PARTS).reshape(1)
    ahead = [(k, (k + 1) % z_count) for k in range(z_count)]
    behind = [(k, (k - 1) % z_count) for k in range(z_count)]
    lines = [list(range(k, z_count, PARTS)) for k in range(PARTS)]

    dma = pltpu.SemaphoreType.DMA
    msg, codes = call(
        dispatch_kernel,
        [((experts, members, 8, half), BF), ((members, tok_rows), jnp.int32)],
        [SM] + [HB] * 3, "dispatch", 3 << 30, 4 << 20,
        scratch=[
            pltpu.VMEM((members, tok_rows), jnp.int32),
            pltpu.VMEM((tok_rows, width), BF),
            pltpu.VMEM((members, tok_rows, width), BF),
            pltpu.VMEM((experts, members, 8, half), BF),
            dma((4,)),
            dma((2,)),
        ],
        out_specs=[HB, VM],
    )(part_index, route_ids[:, :, 0], tokens, out_grad)
    own = lax.all_to_all(
        msg.reshape(places, 8, half), plane, split_axis=0, concat_axis=0, tiled=True
    ).reshape(places * 8, half)
    arrived = (own, lax.ppermute(own, "expert", ahead), lax.ppermute(own, "expert", behind))
    column = lax.dynamic_slice(
        router, (lax.axis_index("member"), 0, lax.axis_index("dp")), (1, width, 1)
    ).reshape(1, width)
    stride = 2 * rows + 32
    share = stride - 2
    block = rows // PARTS
    chunks = width // 128
    whole = ((z_count * share, 128), BF)
    side = pltpu.VMEM((block, width), BF)
    part, kept_own, router_own, first, second = call(
        functools.partial(own_kernel, stride),
        [
            whole,
            ((block, 2 * hidden), BF),
            ((1, width), F32),
            ((width, hidden), BF),
            ((hidden, width), BF),
        ],
        [SM, VM, HB, HB, VM], "expert_own", 1 << 30, 6 << 20,
        scratch=[
            side,
            side,
            pltpu.VMEM((2 * chunks * block, 128), BF),
            pltpu.VMEM((z_count * share - chunks * stride, 128), BF),
            dma((2 * chunks,)),
            dma((2,)),
            dma(()),
        ],
        out_specs=[HB] + [VM] * 4, limit=MOST,
    )(part_index, own, w_in[0, 0], w_out[0, 0], column)
    sides = pltpu.VMEM((2 * block, width), BF)
    part, kept_rest = call(
        functools.partial(rest_kernel, stride),
        [whole, ((2 * block, 2 * hidden), BF)],
        [SM] + [VM] * 6 + [HB], "expert_rest", 2 << 30, 8 << 20,
        scratch=[
            sides,
            sides,
            pltpu.VMEM((4 * chunks * block, 128), BF),
            pltpu.VMEM((chunks * (stride - 2 * rows), 128), BF),
            dma((4 * chunks,)),
            dma((chunks,)),
        ],
        out_specs=[HB, VM], limit=MOST, alias={7: 0},
    )(part_index, *arrived[1:], first, second, column, router_own, part)
    total = lax.psum_scatter(part, "expert", scatter_dimension=0, tiled=True)
    (back,) = call(
        functools.partial(return_kernel, rows),
        [((places * 16, 128), BF)],
        [SM, VM], "to_tokens", 1 << 28, 1 << 20,
        scratch=[pltpu.VMEM((-(-share // 128) * 128, 128), BF)],
        limit=LIMIT,
    )(2 * z.reshape(1), total)
    home = lax.all_to_all(
        back.reshape(places, 16, 128), plane, split_axis=0, concat_axis=0, tiled=True
    ).reshape(places * 16, 128)
    grad_first, grad_second = call(
        weight_kernel,
        [((width, hidden), BF), ((hidden, width), BF)],
        [HB] * 3 + [VM] * 2, "weights", 1 << 30, 6 << 20, limit=LESS,
        scratch=[pltpu.VMEM((rows * 4, half), BF)]
        + [pltpu.VMEM((rows, width), BF)] * 2
        + [dma((2 * PARTS,))],
    )(*arrived, kept_own, kept_rest)
    (compact,) = call(
        collect_kernel,
        [(((members + 1) * tok_rows + places, 128), BF)],
        [VM] * 2, "collect", 1 << 28, 1 << 20, limit=LIMIT,
    )(codes, home)
    line = lax.all_gather(compact, "expert", axis_index_groups=lines)
    moe, token_grad, router_rows = call(
        final_kernel,
        [((members * tok_rows, width), BF), ((tok_rows, width), F32), ((places, width), F32)],
        [SM] + [VM] * 3, "final", 1 << 20, 4 << 20, limit=LIMIT,
    )(
        part_index,
        line,
        lax.ppermute(line, "expert", ahead),
        lax.ppermute(line, "expert", behind),
    )
    router_grad = jnp.transpose(router_rows.reshape(members, experts, width), (0, 2, 1))
    return (
        moe.reshape(members, tok_rows, width),
        token_grad,
        grad_first[None, None],
        grad_second[None, None],
        router_grad,
    )


def solution(mesh):
    in_specs = (
        P(("dp", "member"), None),
        P(None, ("dp", "member"), None),
        P(),
        P("member", "dp", None, "expert"),
        P("member", "dp", "expert", None),
        P(None, ("dp", "member"), None),
    )
    out_specs = (
        P(None, ("dp", "member"), None),
        P(("dp", "member"), None),
        P("member", "dp", None, "expert"),
        P("member", "dp", "expert", None),
        P(),
    )
    return jax.shard_map(shards, mesh=mesh, in_specs=in_specs, out_specs=out_specs, check_vma=False)
```

```python
import functools

import jax
import jax.numpy as jnp
from jax import lax
from jax.experimental import pallas as pl
from jax.experimental.pallas import tpu as pltpu
from jax.sharding import PartitionSpec as P

BF = jnp.bfloat16
F32 = jnp.float32
tanh_scale = 0.7978845608028654
cubic_term = 0.044715
LIMIT = 44 << 20
FULL = 60 << 20
MOST = 50 << 20
LESS = 24 << 20
PARTS = 3
VM = pl.BlockSpec(memory_space=pltpu.VMEM)
HB = pl.BlockSpec(memory_space=pltpu.HBM)
SM = pl.BlockSpec(memory_space=pltpu.SMEM)


def iota(shape, axis):
    return lax.broadcasted_iota(jnp.int32, shape, axis)


def one(mask):
    return jnp.where(mask, 1.0, 0.0).astype(BF)


def to_column(row):
    n = row.shape[1]
    eye = iota((n, n), 0) == iota((n, n), 1)
    return jnp.sum(jnp.where(eye, row, 0), axis=1, keepdims=True)


def dispatch_kernel(
    part_ref, ids_hbm, tok_hbm, grad_hbm, msg_hbm, code_ref, ids_ref, tok_ref, grad_ref, msg_ref, sem, out_sem
):
    loads = [
        pltpu.make_async_copy(src, dst, sem.at[k])
        for k, (src, dst) in enumerate(
            (
                (ids_hbm, ids_ref),
                (tok_hbm, tok_ref),
                (grad_hbm.at[0], grad_ref.at[0]),
                (grad_hbm.at[1], grad_ref.at[1]),
            )
        )
    ]
    for load in loads:
        load.start()
    tok_rows, width = tok_ref.shape
    half = width // 2
    loads[0].wait()
    codes = []
    for m in range(2):
        ids = ids_ref[m : m + 1, :]
        same = to_column(ids) == ids
        earlier = iota((tok_rows, tok_rows), 0) < iota((tok_rows, tok_rows), 1)
        slot = jnp.sum(jnp.where(same & earlier, 1, 0), axis=0, keepdims=True)
        code = ids * 8 + slot
        code_ref[m : m + 1, :] = code
        codes.append(code)
    loads[1].wait()
    token = tok_ref[...]
    stores = []
    for m in range(2):
        loads[2 + m].wait()
        grad = grad_ref[m]
        side = jnp.concatenate(
            [token[:, :half], token[:, half:], grad[:, :half], grad[:, half:]], axis=0
        )
        row = iota((msg_ref.shape[0] * 8, tok_rows), 0)
        kind = lax.shift_right_logical(row & 7, 1)
        code = lax.shift_right_logical(row, 3) * 8 + 2 * part_ref[0] + (row & 1)
        hit = code == codes[m]
        pick = jnp.concatenate([one(hit & (kind == k)) for k in range(4)], axis=1)
        rows = jnp.dot(pick, side, preferred_element_type=F32).astype(BF)
        msg_ref[:, m] = rows.reshape(msg_ref.shape[0], 8, half)
        stores.append(pltpu.make_async_copy(msg_ref.at[:, m], msg_hbm.at[:, m], out_sem.at[m]))
        stores[-1].start()
    for store in stores:
        store.wait()


def nt(a, b):
    return lax.dot_general(a, b, (((1,), (1,)), ((), ())), preferred_element_type=F32)


def tn(a, b):
    return lax.dot_general(a, b, (((0,), (0,)), ((), ())), preferred_element_type=F32)


def sorting():
    p = iota((256, 256), 0)
    source = (
        lax.shift_right_logical(p & 63, 1) * 8 + lax.shift_right_logical(p, 6) * 2 + (p & 1)
    )
    return one(source == iota((256, 256), 1))


def unpack(sort, msg_ref, k, x_ref, g_ref):
    half = msg_ref.shape[1]
    width = 2 * half
    part = jnp.dot(sort, msg_ref[pl.ds(k * 256, 256), :], preferred_element_type=F32).astype(BF)
    here = pl.ds(k * 64, 64)
    x_ref[here, 0:half] = part[0:64]
    x_ref[here, half:width] = part[64:128]
    g_ref[here, 0:half] = part[128:192]
    g_ref[here, half:width] = part[192:256]


def fetch(sources, msg_ref, sem):
    copies = []
    for n, source in enumerate(sources):
        for k in range(2):
            index = 2 * n + k
            copies.append(
                pltpu.make_async_copy(
                    source.at[pl.ds(k * 256, 256)],
                    msg_ref.at[pl.ds(index * 256, 256)],
                    sem.at[index],
                )
            )
    return copies


def wrap(part):
    return jnp.where(part >= PARTS, part - PARTS, part)


def expert_block(rows, stride, index_ref, messages, weights, router_ref, refs, stores):
    part_hbm, kept_ref, x_ref, g_ref, stage_ref, sem = refs
    block = rows // PARTS
    chunks = x_ref.shape[1] // 128
    sort = sorting()
    for n, (_, msg_ref) in enumerate(messages):
        for k in range(2):
            unpack(sort, msg_ref, k, x_ref.at[pl.ds(n * block, block)], g_ref.at[pl.ds(n * block, block)])
    x, g, router = x_ref[...], g_ref[...], router_ref[...]

    def send(value, k):
        for n, (shift, _) in enumerate(messages):
            place = wrap(index_ref[0] + shift) * block
            for c in range(chunks):
                at = (n * 2 + k) * chunks + c
                staged = pl.ds(at * block, block)
                stage_ref[staged, :] = value[
                    n * block : (n + 1) * block, c * 128 : (c + 1) * 128
                ]
                there = pl.ds(pl.multiple_of(place + c * stride + k * rows, 16), block)
                stores.append(
                    pltpu.make_async_copy(stage_ref.at[staged], part_hbm.at[there], sem.at[at])
                )
                stores[-1].start()

    xf = x.astype(F32)
    logit = jnp.sum(xf * router, axis=1, keepdims=True)
    gate = 1.0 / (1.0 + jnp.exp(-logit))
    first, second = weights()
    pre = jnp.dot(x, first, preferred_element_type=F32)
    hidden_grad = nt(g, second)
    tanh_value = jnp.tanh(tanh_scale * (pre + cubic_term * pre * pre * pre))
    act = 0.5 * pre * (1.0 + tanh_value)
    scaled_act = (act * gate).astype(BF)
    send(jnp.dot(scaled_act, second, preferred_element_type=F32).astype(BF), 0)
    slope = 0.5 * (1.0 + tanh_value) + 0.5 * pre * (
        1.0 - tanh_value * tanh_value
    ) * tanh_scale * (1.0 + 3.0 * cubic_term * pre * pre)
    gate_grad = jnp.sum(act * hidden_grad, axis=1, keepdims=True)
    logit_grad = gate_grad * gate * (1.0 - gate)
    pre_grad = (hidden_grad * gate * slope).astype(BF)
    send((nt(pre_grad, first) + logit_grad * router).astype(BF), 1)
    hidden = pre_grad.shape[1]
    kept_ref[:, 0:hidden] = pre_grad
    kept_ref[:, hidden:] = scaled_act
    return jnp.sum(xf * logit_grad, axis=0, keepdims=True)


def own_kernel(
    stride, index_ref, msg_ref, first_hbm, second_hbm, router_ref,
    part_hbm, kept_ref, sum_ref, first_ref, second_ref,
    x_ref, g_ref, stage_ref, zero_ref, sem, load_sem, zero_sem,
):
    loads = [
        pltpu.make_async_copy(first_hbm, first_ref, load_sem.at[0]),
        pltpu.make_async_copy(second_hbm, second_ref, load_sem.at[1]),
    ]
    for load in loads:
        load.start()
    zero_ref[...] = jnp.zeros(zero_ref.shape, BF)
    there = pl.ds(x_ref.shape[1] // 128 * stride, zero_ref.shape[0])
    stores = [pltpu.make_async_copy(zero_ref, part_hbm.at[there], zero_sem)]
    stores[0].start()

    def weights():
        for load in loads:
            load.wait()
        return first_ref[...], second_ref[...]

    sum_ref[...] = expert_block(
        PARTS * x_ref.shape[0], stride, index_ref, [(0, msg_ref)], weights, router_ref,
        (part_hbm, kept_ref, x_ref, g_ref, stage_ref, sem), stores,
    )
    for store in stores:
        store.wait()


def rest_kernel(
    stride, index_ref, up_ref, down_ref, first_ref, second_ref, router_ref, before_ref, _,
    part_hbm, kept_ref, x_ref, g_ref, stage_ref, tail_ref, sem, tail_sem,
):
    rows = PARTS * x_ref.shape[0] // 2
    stores = []
    router_sum = before_ref[...] + expert_block(
        rows, stride, index_ref, [(2, up_ref), (1, down_ref)],
        lambda: (first_ref[...], second_ref[...]), router_ref,
        (part_hbm, kept_ref, x_ref, g_ref, stage_ref, sem), stores,
    )
    tail = stride - 2 * rows
    for c in range(x_ref.shape[1] // 128):
        lanes = slice(c * 128, (c + 1) * 128)
        row = jnp.where(iota((tail, 128), 0) == 0, router_sum[:, lanes], 0.0)
        staged = pl.ds(c * tail, tail)
        tail_ref[staged, :] = row.astype(BF)
        there = pl.ds(c * stride + 2 * rows, tail)
        stores.append(
            pltpu.make_async_copy(tail_ref.at[staged], part_hbm.at[there], tail_sem.at[c])
        )
        stores[-1].start()
    for store in stores:
        store.wait()


def weight_kernel(
    own_hbm, up_hbm, down_hbm, own_ref, rest_ref,
    first_ref, second_ref, msg_ref, x_ref, g_ref, sem,
):
    loads = fetch((own_hbm, up_hbm, down_hbm), msg_ref, sem)
    for load in loads:
        load.start()
    sort = sorting()
    for k, load in enumerate(loads):
        load.wait()
        unpack(sort, msg_ref, k, x_ref, g_ref)
    kept = jnp.concatenate([own_ref[...], rest_ref[...]], axis=0)
    pre_grad, scaled_act = jnp.split(kept, 2, axis=1)
    first_ref[...] = tn(x_ref[...], pre_grad).astype(BF)
    second_ref[...] = tn(scaled_act, g_ref[...]).astype(BF)


def return_kernel(rows, shift_ref, sum_ref, msg_ref, hold_ref):
    depth = hold_ref.shape[0]
    given = sum_ref.shape[0]
    base = given // 16 * 16
    hold_ref[pl.ds(base, depth - base), :] = jnp.zeros((depth - base, 128), BF)
    hold_ref[pl.ds(0, given), :] = sum_ref[...]
    shift = shift_ref[0]
    held = hold_ref[...]
    block = 256
    for b in range(msg_ref.shape[0] // block):
        row = iota((block, depth), 0) + b * block
        source = lax.shift_right_logical(row, 4)
        r = row & 15
        slot = jnp.where(r < 6, r, r - 6)
        want = lax.shift_right_logical(slot, 1) * (rows // PARTS) + source * 2 + (slot & 1)
        want = jnp.where(r < 6, want, rows + want)
        want = jnp.where(r < 12, want, jnp.where(r == 12, 2 * rows, -depth)) + shift
        msg_ref[pl.ds(b * block, block), :] = jnp.dot(
            one(want == iota((block, depth), 1)), held, preferred_element_type=F32
        ).astype(BF)


def collect_kernel(code_ref, msg_ref, out_ref):
    held = msg_ref[...]
    depth = held.shape[0]
    tok_rows = code_ref.shape[1]
    picked = None
    for m in range(2):
        code = to_column(code_ref[m : m + 1, :])
        want = (lax.shift_right_logical(code, 3) * 2 + m) * 16 + (code & 7)
        lane = iota((tok_rows, depth), 1)
        out_ref[pl.ds(m * tok_rows, tok_rows), :] = jnp.dot(
            one(lane == want), held, preferred_element_type=F32
        ).astype(BF)
        pick = one(lane == want + 6)
        picked = pick if picked is None else picked + pick
    out_ref[pl.ds(2 * tok_rows, tok_rows), :] = jnp.dot(picked, held, preferred_element_type=F32).astype(BF)
    n = depth // 16
    row = iota((n, depth), 0)
    want = ((row & (n // 2 - 1)) * 2 + jnp.where(row >= n // 2, 1, 0)) * 16 + 12
    out_ref[pl.ds(3 * tok_rows, n), :] = jnp.dot(
        one(iota((n, depth), 1) == want), held, preferred_element_type=F32
    ).astype(BF)


def final_kernel(part_ref, own_ref, up_ref, down_ref, moe_ref, token_ref, router_ref):
    tok_rows, width = token_ref.shape
    for ref, shift in ((own_ref, 0), (up_ref, 2), (down_ref, 1)):
        part = wrap(part_ref[0] + shift)
        for k in range(ref.shape[0]):

            @pl.when(part + PARTS * k < width // 128)
            def _():
                lanes = pl.ds(pl.multiple_of((part + PARTS * k) * 128, 128), 128)
                moe_ref[:, lanes] = ref[k, 0 : 2 * tok_rows, :]
                token_ref[:, lanes] = ref[k, 2 * tok_rows : 3 * tok_rows, :].astype(F32)
                router_ref[:, lanes] = ref[k, 3 * tok_rows :, :].astype(F32)


def call(kernel, out, specs, name, flops, size, scratch=(), out_specs=None, limit=FULL, alias=None):
    return pl.pallas_call(
        kernel,
        out_shape=[jax.ShapeDtypeStruct(s, d) for s, d in out],
        in_specs=specs,
        out_specs=out_specs or [VM] * len(out),
        scratch_shapes=list(scratch),
        input_output_aliases=alias or {},
        compiler_params=pltpu.CompilerParams(vmem_limit_bytes=limit),
        cost_estimate=pl.CostEstimate(flops=flops, bytes_accessed=size, transcendentals=0),
        name=name,
    )


def shards(tokens, route_ids, router, w_in, w_out, out_grad):
    members, tok_rows = route_ids.shape[0], route_ids.shape[1]
    experts, width = router.shape[2], router.shape[1]
    hidden = w_in.shape[3]
    places = experts * members
    capacity = 3 * tok_rows // (2 * experts)
    rows = places * capacity
    half = width // 2
    plane = ("dp", "member")
    z_count = lax.axis_size("expert")
    z = lax.axis_index("expert")
    part_index = (z % PARTS).reshape(1)
    ahead = [(k, (k + 1) % z_count) for k in range(z_count)]
    behind = [(k, (k - 1) % z_count) for k in range(z_count)]
    lines = [list(range(k, z_count, PARTS)) for k in range(PARTS)]

    dma = pltpu.SemaphoreType.DMA
    msg, codes = call(
        dispatch_kernel,
        [((experts, members, 8, half), BF), ((members, tok_rows), jnp.int32)],
        [SM] + [HB] * 3, "dispatch", 3 << 30, 4 << 20,
        scratch=[
            pltpu.VMEM((members, tok_rows), jnp.int32),
            pltpu.VMEM((tok_rows, width), BF),
            pltpu.VMEM((members, tok_rows, width), BF),
            pltpu.VMEM((experts, members, 8, half), BF),
            dma((4,)),
            dma((2,)),
        ],
        out_specs=[HB, VM],
    )(part_index, route_ids[:, :, 0], tokens, out_grad)
    own = lax.all_to_all(
        msg.reshape(places, 8, half), plane, split_axis=0, concat_axis=0, tiled=True
    ).reshape(places * 8, half)
    arrived = (own, lax.ppermute(own, "expert", ahead), lax.ppermute(own, "expert", behind))
    column = lax.dynamic_slice(
        router, (lax.axis_index("member"), 0, lax.axis_index("dp")), (1, width, 1)
    ).reshape(1, width)
    stride = 2 * rows + 32
    share = stride - 2
    block = rows // PARTS
    chunks = width // 128
    whole = ((z_count * share, 128), BF)
    side = pltpu.VMEM((block, width), BF)
    part, kept_own, router_own, first, second = call(
        functools.partial(own_kernel, stride),
        [
            whole,
            ((block, 2 * hidden), BF),
            ((1, width), F32),
            ((width, hidden), BF),
            ((hidden, width), BF),
        ],
        [SM, VM, HB, HB, VM], "expert_own", 1 << 30, 6 << 20,
        scratch=[
            side,
            side,
            pltpu.VMEM((2 * chunks * block, 128), BF),
            pltpu.VMEM((z_count * share - chunks * stride, 128), BF),
            dma((2 * chunks,)),
            dma((2,)),
            dma(()),
        ],
        out_specs=[HB] + [VM] * 4, limit=MOST,
    )(part_index, own, w_in[0, 0], w_out[0, 0], column)
    sides = pltpu.VMEM((2 * block, width), BF)
    part, kept_rest = call(
        functools.partial(rest_kernel, stride),
        [whole, ((2 * block, 2 * hidden), BF)],
        [SM] + [VM] * 6 + [HB], "expert_rest", 2 << 30, 8 << 20,
        scratch=[
            sides,
            sides,
            pltpu.VMEM((4 * chunks * block, 128), BF),
            pltpu.VMEM((chunks * (stride - 2 * rows), 128), BF),
            dma((4 * chunks,)),
            dma((chunks,)),
        ],
        out_specs=[HB, VM], limit=MOST, alias={7: 0},
    )(part_index, *arrived[1:], first, second, column, router_own, part)
    total = lax.psum_scatter(part, "expert", scatter_dimension=0, tiled=True)
    (back,) = call(
        functools.partial(return_kernel, rows),
        [((places * 16, 128), BF)],
        [SM, VM], "to_tokens", 1 << 28, 1 << 20,
        scratch=[pltpu.VMEM((-(-share // 128) * 128, 128), BF)],
        limit=LIMIT,
    )(2 * z.reshape(1), total)
    home = lax.all_to_all(
        back.reshape(places, 16, 128), plane, split_axis=0, concat_axis=0, tiled=True
    ).reshape(places * 16, 128)
    grad_first, grad_second = call(
        weight_kernel,
        [((width, hidden), BF), ((hidden, width), BF)],
        [HB] * 3 + [VM] * 2, "weights", 1 << 30, 6 << 20, limit=LESS,
        scratch=[pltpu.VMEM((rows * 4, half), BF)]
        + [pltpu.VMEM((rows, width), BF)] * 2
        + [dma((2 * PARTS,))],
    )(*arrived, kept_own, kept_rest)
    home, grad_first, grad_second = lax.optimization_barrier((home, grad_first, grad_second))
    (compact,) = call(
        collect_kernel,
        [(((members + 1) * tok_rows + places, 128), BF)],
        [VM] * 2, "collect", 1 << 28, 1 << 20, limit=LIMIT,
    )(codes, home)
    line = lax.all_gather(compact, "expert", axis_index_groups=lines)
    moe, token_grad, router_rows = call(
        final_kernel,
        [((members * tok_rows, width), BF), ((tok_rows, width), F32), ((places, width), F32)],
        [SM] + [VM] * 3, "final", 1 << 20, 4 << 20, limit=LIMIT,
    )(
        part_index,
        line,
        lax.ppermute(line, "expert", ahead),
        lax.ppermute(line, "expert", behind),
    )
    router_grad = jnp.transpose(router_rows.reshape(members, experts, width), (0, 2, 1))
    return (
        moe.reshape(members, tok_rows, width),
        token_grad,
        grad_first[None, None],
        grad_second[None, None],
        router_grad,
    )


def solution(mesh):
    in_specs = (
        P(("dp", "member"), None),
        P(None, ("dp", "member"), None),
        P(),
        P("member", "dp", None, "expert"),
        P("member", "dp", "expert", None),
        P(None, ("dp", "member"), None),
    )
    out_specs = (
        P(None, ("dp", "member"), None),
        P(("dp", "member"), None),
        P("member", "dp", None, "expert"),
        P("member", "dp", "expert", None),
        P(),
    )
    return jax.shard_map(shards, mesh=mesh, in_specs=in_specs, out_specs=out_specs, check_vma=False)
```

```python
import functools

import jax
import jax.numpy as jnp
from jax import lax
from jax.experimental import pallas as pl
from jax.experimental.pallas import tpu as pltpu
from jax.sharding import PartitionSpec as P

BF = jnp.bfloat16
F32 = jnp.float32
tanh_scale = 0.7978845608028654
cubic_term = 0.044715
LIMIT = 44 << 20
FULL = 60 << 20
MOST = 50 << 20
LESS = 24 << 20
PARTS = 3
VM = pl.BlockSpec(memory_space=pltpu.VMEM)
HB = pl.BlockSpec(memory_space=pltpu.HBM)
SM = pl.BlockSpec(memory_space=pltpu.SMEM)


def iota(shape, axis):
    return lax.broadcasted_iota(jnp.int32, shape, axis)


def one(mask):
    return jnp.where(mask, 1.0, 0.0).astype(BF)


def to_column(row):
    n = row.shape[1]
    eye = iota((n, n), 0) == iota((n, n), 1)
    return jnp.sum(jnp.where(eye, row, 0), axis=1, keepdims=True)


def dispatch_kernel(
    part_ref, ids_hbm, tok_hbm, grad_hbm, msg_hbm, code_ref, ids_ref, tok_ref, grad_ref, msg_ref, sem, out_sem
):
    loads = [
        pltpu.make_async_copy(src, dst, sem.at[k])
        for k, (src, dst) in enumerate(
            (
                (ids_hbm, ids_ref),
                (tok_hbm, tok_ref),
                (grad_hbm.at[0], grad_ref.at[0]),
                (grad_hbm.at[1], grad_ref.at[1]),
            )
        )
    ]
    for load in loads:
        load.start()
    tok_rows, width = tok_ref.shape
    half = width // 2
    loads[0].wait()
    codes = []
    for m in range(2):
        ids = ids_ref[m : m + 1, :]
        same = to_column(ids) == ids
        earlier = iota((tok_rows, tok_rows), 0) < iota((tok_rows, tok_rows), 1)
        slot = jnp.sum(jnp.where(same & earlier, 1, 0), axis=0, keepdims=True)
        code = ids * 8 + slot
        code_ref[m : m + 1, :] = code
        codes.append(code)
    loads[1].wait()
    token = tok_ref[...]
    stores = []
    for m in range(2):
        loads[2 + m].wait()
        grad = grad_ref[m]
        side = jnp.concatenate(
            [token[:, :half], token[:, half:], grad[:, :half], grad[:, half:]], axis=0
        )
        row = iota((msg_ref.shape[0] * 8, tok_rows), 0)
        kind = lax.shift_right_logical(row & 7, 1)
        code = lax.shift_right_logical(row, 3) * 8 + 2 * part_ref[0] + (row & 1)
        hit = code == codes[m]
        pick = jnp.concatenate([one(hit & (kind == k)) for k in range(4)], axis=1)
        rows = jnp.dot(pick, side, preferred_element_type=F32).astype(BF)
        msg_ref[:, m] = rows.reshape(msg_ref.shape[0], 8, half)
        stores.append(pltpu.make_async_copy(msg_ref.at[:, m], msg_hbm.at[:, m], out_sem.at[m]))
        stores[-1].start()
    for store in stores:
        store.wait()


def nt(a, b):
    return lax.dot_general(a, b, (((1,), (1,)), ((), ())), preferred_element_type=F32)


def tn(a, b):
    return lax.dot_general(a, b, (((0,), (0,)), ((), ())), preferred_element_type=F32)


def sorting():
    p = iota((256, 256), 0)
    source = (
        lax.shift_right_logical(p & 63, 1) * 8 + lax.shift_right_logical(p, 6) * 2 + (p & 1)
    )
    return one(source == iota((256, 256), 1))


def unpack(sort, msg_ref, k, x_ref, g_ref):
    half = msg_ref.shape[1]
    width = 2 * half
    part = jnp.dot(sort, msg_ref[pl.ds(k * 256, 256), :], preferred_element_type=F32).astype(BF)
    here = pl.ds(k * 64, 64)
    x_ref[here, 0:half] = part[0:64]
    x_ref[here, half:width] = part[64:128]
    g_ref[here, 0:half] = part[128:192]
    g_ref[here, half:width] = part[192:256]


def fetch(sources, msg_ref, sem):
    copies = []
    for n, source in enumerate(sources):
        for k in range(2):
            index = 2 * n + k
            copies.append(
                pltpu.make_async_copy(
                    source.at[pl.ds(k * 256, 256)],
                    msg_ref.at[pl.ds(index * 256, 256)],
                    sem.at[index],
                )
            )
    return copies


def wrap(part):
    return jnp.where(part >= PARTS, part - PARTS, part)


def expert_block(rows, stride, index_ref, messages, weights, router_ref, refs, stores):
    part_hbm, kept_ref, x_ref, g_ref, stage_ref, sem = refs
    block = rows // PARTS
    places = -(-part_hbm.shape[0] // stride)
    last = x_ref.shape[1] // 128 - 1
    sort = sorting()
    for n, (_, msg_ref) in enumerate(messages):
        for k in range(2):
            unpack(sort, msg_ref, k, x_ref.at[pl.ds(n * block, block)], g_ref.at[pl.ds(n * block, block)])
    x, g, router = x_ref[...], g_ref[...], router_ref[...]

    def send(value, k):
        for n, (shift, _) in enumerate(messages):
            place = wrap(index_ref[0] + shift) * block
            for c in range(places):
                staged = pl.ds(((n * 2 + k) * (last + 1) + min(c, last)) * block, block)
                if c <= last:
                    stage_ref[staged, :] = value[
                        n * block : (n + 1) * block, c * 128 : (c + 1) * 128
                    ]
                there = pl.ds(pl.multiple_of(place + c * stride + k * rows, 16), block)
                at = (n * 2 + k) * places + c
                stores.append(
                    pltpu.make_async_copy(stage_ref.at[staged], part_hbm.at[there], sem.at[at])
                )
                stores[-1].start()

    xf = x.astype(F32)
    logit = jnp.sum(xf * router, axis=1, keepdims=True)
    gate = 1.0 / (1.0 + jnp.exp(-logit))
    first, second = weights()
    pre = jnp.dot(x, first, preferred_element_type=F32)
    hidden_grad = nt(g, second)
    tanh_value = jnp.tanh(tanh_scale * (pre + cubic_term * pre * pre * pre))
    act = 0.5 * pre * (1.0 + tanh_value)
    scaled_act = (act * gate).astype(BF)
    send(jnp.dot(scaled_act, second, preferred_element_type=F32).astype(BF), 0)
    slope = 0.5 * (1.0 + tanh_value) + 0.5 * pre * (
        1.0 - tanh_value * tanh_value
    ) * tanh_scale * (1.0 + 3.0 * cubic_term * pre * pre)
    gate_grad = jnp.sum(act * hidden_grad, axis=1, keepdims=True)
    logit_grad = gate_grad * gate * (1.0 - gate)
    pre_grad = (hidden_grad * gate * slope).astype(BF)
    send((nt(pre_grad, first) + logit_grad * router).astype(BF), 1)
    hidden = pre_grad.shape[1]
    kept_ref[:, 0:hidden] = pre_grad
    kept_ref[:, hidden:] = scaled_act
    return jnp.sum(xf * logit_grad, axis=0, keepdims=True)


def own_kernel(
    stride, index_ref, msg_ref, first_hbm, second_hbm, router_ref,
    part_hbm, kept_ref, sum_ref, first_ref, second_ref,
    x_ref, g_ref, stage_ref, sem, load_sem,
):
    loads = [
        pltpu.make_async_copy(first_hbm, first_ref, load_sem.at[0]),
        pltpu.make_async_copy(second_hbm, second_ref, load_sem.at[1]),
    ]
    for load in loads:
        load.start()
    stores = []

    def weights():
        for load in loads:
            load.wait()
        return first_ref[...], second_ref[...]

    sum_ref[...] = expert_block(
        PARTS * x_ref.shape[0], stride, index_ref, [(0, msg_ref)], weights, router_ref,
        (part_hbm, kept_ref, x_ref, g_ref, stage_ref, sem), stores,
    )
    for store in stores:
        store.wait()


def rest_kernel(
    stride, index_ref, up_ref, down_ref, first_ref, second_ref, router_ref, before_ref, _,
    part_hbm, kept_ref, x_ref, g_ref, stage_ref, tail_ref, sem, tail_sem,
):
    rows = PARTS * x_ref.shape[0] // 2
    stores = []
    router_sum = before_ref[...] + expert_block(
        rows, stride, index_ref, [(2, up_ref), (1, down_ref)],
        lambda: (first_ref[...], second_ref[...]), router_ref,
        (part_hbm, kept_ref, x_ref, g_ref, stage_ref, sem), stores,
    )
    tail = stride - 2 * rows
    last = x_ref.shape[1] // 128 - 1
    total = part_hbm.shape[0]
    for c in range(-(-total // stride)):
        if c <= last:
            row = jnp.where(
                iota((tail, 128), 0) == 0, router_sum[:, c * 128 : (c + 1) * 128], 0.0
            )
            tail_ref[pl.ds(c * tail, tail), :] = row.astype(BF)
        start = c * stride + 2 * rows
        size = min(tail, total - start)
        stores.append(
            pltpu.make_async_copy(
                tail_ref.at[pl.ds(min(c, last) * tail, size)],
                part_hbm.at[pl.ds(start, size)],
                tail_sem.at[c],
            )
        )
        stores[-1].start()
    for store in stores:
        store.wait()


def weight_kernel(
    own_hbm, up_hbm, down_hbm, own_ref, rest_ref,
    first_ref, second_ref, msg_ref, x_ref, g_ref, sem,
):
    loads = fetch((own_hbm, up_hbm, down_hbm), msg_ref, sem)
    for load in loads:
        load.start()
    sort = sorting()
    for k, load in enumerate(loads):
        load.wait()
        unpack(sort, msg_ref, k, x_ref, g_ref)
    kept = jnp.concatenate([own_ref[...], rest_ref[...]], axis=0)
    pre_grad, scaled_act = jnp.split(kept, 2, axis=1)
    first_ref[...] = tn(x_ref[...], pre_grad).astype(BF)
    second_ref[...] = tn(scaled_act, g_ref[...]).astype(BF)


def return_kernel(rows, shift_ref, sum_ref, msg_ref, hold_ref):
    depth = hold_ref.shape[0]
    given = sum_ref.shape[0]
    base = given // 16 * 16
    hold_ref[pl.ds(base, depth - base), :] = jnp.zeros((depth - base, 128), BF)
    hold_ref[pl.ds(0, given), :] = sum_ref[...]
    shift = shift_ref[0]
    held = hold_ref[...]
    block = 256
    for b in range(msg_ref.shape[0] // block):
        row = iota((block, depth), 0) + b * block
        source = lax.shift_right_logical(row, 4)
        r = row & 15
        slot = jnp.where(r < 6, r, r - 6)
        want = lax.shift_right_logical(slot, 1) * (rows // PARTS) + source * 2 + (slot & 1)
        want = jnp.where(r < 6, want, rows + want)
        want = jnp.where(r < 12, want, jnp.where(r == 12, 2 * rows, -depth)) + shift
        msg_ref[pl.ds(b * block, block), :] = jnp.dot(
            one(want == iota((block, depth), 1)), held, preferred_element_type=F32
        ).astype(BF)


def collect_kernel(code_ref, msg_ref, out_ref):
    held = msg_ref[...]
    depth = held.shape[0]
    tok_rows = code_ref.shape[1]
    picked = None
    for m in range(2):
        code = to_column(code_ref[m : m + 1, :])
        want = (lax.shift_right_logical(code, 3) * 2 + m) * 16 + (code & 7)
        lane = iota((tok_rows, depth), 1)
        out_ref[pl.ds(m * tok_rows, tok_rows), :] = jnp.dot(
            one(lane == want), held, preferred_element_type=F32
        ).astype(BF)
        pick = one(lane == want + 6)
        picked = pick if picked is None else picked + pick
    out_ref[pl.ds(2 * tok_rows, tok_rows), :] = jnp.dot(picked, held, preferred_element_type=F32).astype(BF)
    n = depth // 16
    row = iota((n, depth), 0)
    want = ((row & (n // 2 - 1)) * 2 + jnp.where(row >= n // 2, 1, 0)) * 16 + 12
    out_ref[pl.ds(3 * tok_rows, n), :] = jnp.dot(
        one(iota((n, depth), 1) == want), held, preferred_element_type=F32
    ).astype(BF)


def final_kernel(part_ref, own_ref, up_ref, down_ref, moe_ref, token_ref, router_ref):
    tok_rows, width = token_ref.shape

    def place(block, lanes):
        moe_ref[:, lanes] = block[0 : 2 * tok_rows, :]
        token_ref[:, lanes] = block[2 * tok_rows : 3 * tok_rows, :].astype(F32)
        router_ref[:, lanes] = block[3 * tok_rows :, :].astype(F32)

    for ref, shift in ((own_ref, 0), (up_ref, 2), (down_ref, 1)):
        part = wrap(part_ref[0] + shift)
        for k in range(up_ref.shape[0]):
            lanes = pl.ds(pl.multiple_of((part + PARTS * k) * 128, 128), 128)
            place(ref.at[k], lanes)
    place(own_ref.at[own_ref.shape[0] - 1], slice(width - 128, width))


def call(kernel, out, specs, name, flops, size, scratch=(), out_specs=None, limit=FULL, alias=None):
    return pl.pallas_call(
        kernel,
        out_shape=[jax.ShapeDtypeStruct(s, d) for s, d in out],
        in_specs=specs,
        out_specs=out_specs or [VM] * len(out),
        scratch_shapes=list(scratch),
        input_output_aliases=alias or {},
        compiler_params=pltpu.CompilerParams(vmem_limit_bytes=limit),
        cost_estimate=pl.CostEstimate(flops=flops, bytes_accessed=size, transcendentals=0),
        name=name,
    )


def shards(tokens, route_ids, router, w_in, w_out, out_grad):
    members, tok_rows = route_ids.shape[0], route_ids.shape[1]
    experts, width = router.shape[2], router.shape[1]
    hidden = w_in.shape[3]
    places = experts * members
    capacity = 3 * tok_rows // (2 * experts)
    rows = places * capacity
    half = width // 2
    plane = ("dp", "member")
    z_count = lax.axis_size("expert")
    z = lax.axis_index("expert")
    part_index = (z % PARTS).reshape(1)
    ahead = [(k, (k + 1) % z_count) for k in range(z_count)]
    behind = [(k, (k - 1) % z_count) for k in range(z_count)]
    lines = [list(range(k, z_count, PARTS)) for k in range(PARTS)]

    dma = pltpu.SemaphoreType.DMA
    msg, codes = call(
        dispatch_kernel,
        [((experts, members, 8, half), BF), ((members, tok_rows), jnp.int32)],
        [SM] + [HB] * 3, "dispatch", 3 << 30, 4 << 20,
        scratch=[
            pltpu.VMEM((members, tok_rows), jnp.int32),
            pltpu.VMEM((tok_rows, width), BF),
            pltpu.VMEM((members, tok_rows, width), BF),
            pltpu.VMEM((experts, members, 8, half), BF),
            dma((4,)),
            dma((2,)),
        ],
        out_specs=[HB, VM],
    )(part_index, route_ids[:, :, 0], tokens, out_grad)
    own = lax.all_to_all(
        msg.reshape(places, 8, half), plane, split_axis=0, concat_axis=0, tiled=True
    ).reshape(places * 8, half)
    arrived = (own, lax.ppermute(own, "expert", ahead), lax.ppermute(own, "expert", behind))
    column = lax.dynamic_slice(
        router, (lax.axis_index("member"), 0, lax.axis_index("dp")), (1, width, 1)
    ).reshape(1, width)
    stride = 2 * rows + 32
    share = stride - 2
    block = rows // PARTS
    chunks = width // 128
    whole = ((z_count * share, 128), BF)
    side = pltpu.VMEM((block, width), BF)
    part, kept_own, router_own, first, second = call(
        functools.partial(own_kernel, stride),
        [
            whole,
            ((block, 2 * hidden), BF),
            ((1, width), F32),
            ((width, hidden), BF),
            ((hidden, width), BF),
        ],
        [SM, VM, HB, HB, VM], "expert_own", 1 << 30, 6 << 20,
        scratch=[
            side,
            side,
            pltpu.VMEM((2 * chunks * block, 128), BF),
            dma((2 * z_count,)),
            dma((2,)),
        ],
        out_specs=[HB] + [VM] * 4, limit=MOST,
    )(part_index, own, w_in[0, 0], w_out[0, 0], column)
    sides = pltpu.VMEM((2 * block, width), BF)
    part, kept_rest = call(
        functools.partial(rest_kernel, stride),
        [whole, ((2 * block, 2 * hidden), BF)],
        [SM] + [VM] * 6 + [HB], "expert_rest", 2 << 30, 8 << 20,
        scratch=[
            sides,
            sides,
            pltpu.VMEM((4 * chunks * block, 128), BF),
            pltpu.VMEM((chunks * (stride - 2 * rows), 128), BF),
            dma((4 * z_count,)),
            dma((z_count,)),
        ],
        out_specs=[HB, VM], limit=MOST, alias={7: 0},
    )(part_index, *arrived[1:], first, second, column, router_own, part)
    total = lax.psum_scatter(part, "expert", scatter_dimension=0, tiled=True)
    (back,) = call(
        functools.partial(return_kernel, rows),
        [((places * 16, 128), BF)],
        [SM, VM], "to_tokens", 1 << 28, 1 << 20,
        scratch=[pltpu.VMEM((-(-share // 128) * 128, 128), BF)],
        limit=LIMIT,
    )(2 * z.reshape(1), total)
    home = lax.all_to_all(
        back.reshape(places, 16, 128), plane, split_axis=0, concat_axis=0, tiled=True
    ).reshape(places * 16, 128)
    grad_first, grad_second = call(
        weight_kernel,
        [((width, hidden), BF), ((hidden, width), BF)],
        [HB] * 3 + [VM] * 2, "weights", 1 << 30, 6 << 20, limit=LESS,
        scratch=[pltpu.VMEM((rows * 4, half), BF)]
        + [pltpu.VMEM((rows, width), BF)] * 2
        + [dma((2 * PARTS,))],
    )(*arrived, kept_own, kept_rest)
    (compact,) = call(
        collect_kernel,
        [(((members + 1) * tok_rows + places, 128), BF)],
        [VM] * 2, "collect", 1 << 28, 1 << 20, limit=LIMIT,
    )(codes, home)
    line = lax.all_gather(compact, "expert", axis_index_groups=lines)
    moe, token_grad, router_rows = call(
        final_kernel,
        [((members * tok_rows, width), BF), ((tok_rows, width), F32), ((places, width), F32)],
        [SM] + [VM] * 3, "final", 1 << 20, 4 << 20, limit=LIMIT,
    )(
        part_index,
        line,
        lax.ppermute(line[:-1], "expert", ahead),
        lax.ppermute(line[:-1], "expert", behind),
    )
    router_grad = jnp.transpose(router_rows.reshape(members, experts, width), (0, 2, 1))
    return (
        moe.reshape(members, tok_rows, width),
        token_grad,
        grad_first[None, None],
        grad_second[None, None],
        router_grad,
    )


def solution(mesh):
    in_specs = (
        P(("dp", "member"), None),
        P(None, ("dp", "member"), None),
        P(),
        P("member", "dp", None, "expert"),
        P("member", "dp", "expert", None),
        P(None, ("dp", "member"), None),
    )
    out_specs = (
        P(None, ("dp", "member"), None),
        P(("dp", "member"), None),
        P("member", "dp", None, "expert"),
        P("member", "dp", "expert", None),
        P(),
    )
    return jax.shard_map(shards, mesh=mesh, in_specs=in_specs, out_specs=out_specs, check_vma=False)
```

```python
import functools

import jax
import jax.numpy as jnp
from jax import lax
from jax.experimental import pallas as pl
from jax.experimental.pallas import tpu as pltpu
from jax.sharding import PartitionSpec as P

BF = jnp.bfloat16
F32 = jnp.float32
tanh_scale = 0.7978845608028654
cubic_term = 0.044715
LIMIT = 44 << 20
FULL = 60 << 20
MOST = 50 << 20
LESS = 24 << 20
PARTS = 3
VM = pl.BlockSpec(memory_space=pltpu.VMEM)
HB = pl.BlockSpec(memory_space=pltpu.HBM)
SM = pl.BlockSpec(memory_space=pltpu.SMEM)


def iota(shape, axis):
    return lax.broadcasted_iota(jnp.int32, shape, axis)


def one(mask):
    return jnp.where(mask, 1.0, 0.0).astype(BF)


def to_column(row):
    n = row.shape[1]
    eye = iota((n, n), 0) == iota((n, n), 1)
    return jnp.sum(jnp.where(eye, row, 0), axis=1, keepdims=True)


def dispatch_kernel(
    part_ref, ids_hbm, tok_hbm, grad_hbm, msg_hbm, code_ref, ids_ref, tok_ref, grad_ref, msg_ref, sem, out_sem
):
    loads = [
        pltpu.make_async_copy(src, dst, sem.at[k])
        for k, (src, dst) in enumerate(
            (
                (ids_hbm, ids_ref),
                (tok_hbm, tok_ref),
                (grad_hbm.at[0], grad_ref.at[0]),
                (grad_hbm.at[1], grad_ref.at[1]),
            )
        )
    ]
    for load in loads:
        load.start()
    tok_rows, width = tok_ref.shape
    half = width // 2
    loads[0].wait()
    codes = []
    for m in range(2):
        ids = ids_ref[m : m + 1, :]
        same = to_column(ids) == ids
        earlier = iota((tok_rows, tok_rows), 0) < iota((tok_rows, tok_rows), 1)
        slot = jnp.sum(jnp.where(same & earlier, 1, 0), axis=0, keepdims=True)
        code = ids * 8 + slot
        code_ref[m : m + 1, :] = code
        codes.append(code)
    loads[1].wait()
    token = tok_ref[...]
    stores = []
    for m in range(2):
        loads[2 + m].wait()
        grad = grad_ref[m]
        side = jnp.concatenate(
            [token[:, :half], token[:, half:], grad[:, :half], grad[:, half:]], axis=0
        )
        row = iota((msg_ref.shape[0] * 8, tok_rows), 0)
        kind = lax.shift_right_logical(row & 7, 1)
        code = lax.shift_right_logical(row, 3) * 8 + 2 * part_ref[0] + (row & 1)
        hit = code == codes[m]
        pick = jnp.concatenate([one(hit & (kind == k)) for k in range(4)], axis=1)
        rows = jnp.dot(pick, side, preferred_element_type=F32).astype(BF)
        msg_ref[:, m] = rows.reshape(msg_ref.shape[0], 8, half)
        stores.append(pltpu.make_async_copy(msg_ref.at[:, m], msg_hbm.at[:, m], out_sem.at[m]))
        stores[-1].start()
    for store in stores:
        store.wait()


def nt(a, b):
    return lax.dot_general(a, b, (((1,), (1,)), ((), ())), preferred_element_type=F32)


def tn(a, b):
    return lax.dot_general(a, b, (((0,), (0,)), ((), ())), preferred_element_type=F32)


def sorting():
    p = iota((256, 256), 0)
    source = (
        lax.shift_right_logical(p & 63, 1) * 8 + lax.shift_right_logical(p, 6) * 2 + (p & 1)
    )
    return one(source == iota((256, 256), 1))


def unpack(sort, msg_ref, k, x_ref, g_ref):
    half = msg_ref.shape[1]
    width = 2 * half
    part = jnp.dot(sort, msg_ref[pl.ds(k * 256, 256), :], preferred_element_type=F32).astype(BF)
    here = pl.ds(k * 64, 64)
    x_ref[here, 0:half] = part[0:64]
    x_ref[here, half:width] = part[64:128]
    g_ref[here, 0:half] = part[128:192]
    g_ref[here, half:width] = part[192:256]


def fetch(sources, msg_ref, sem):
    copies = []
    for n, source in enumerate(sources):
        for k in range(2):
            index = 2 * n + k
            copies.append(
                pltpu.make_async_copy(
                    source.at[pl.ds(k * 256, 256)],
                    msg_ref.at[pl.ds(index * 256, 256)],
                    sem.at[index],
                )
            )
    return copies


def wrap(part):
    return jnp.where(part >= PARTS, part - PARTS, part)


def expert_block(rows, stride, index_ref, messages, weights, router_ref, refs, stores):
    part_hbm, kept_ref, x_ref, g_ref, stage_ref, sem = refs
    block = rows // PARTS
    places = -(-part_hbm.shape[0] // stride)
    last = x_ref.shape[1] // 128 - 1
    sort = sorting()
    for n, (_, msg_ref) in enumerate(messages):
        for k in range(2):
            unpack(sort, msg_ref, k, x_ref.at[pl.ds(n * block, block)], g_ref.at[pl.ds(n * block, block)])
    x, g, router = x_ref[...], g_ref[...], router_ref[...]

    def send(value, k):
        for n, (shift, _) in enumerate(messages):
            place = wrap(index_ref[0] + shift) * block
            for c in range(places):
                staged = pl.ds(((n * 2 + k) * (last + 1) + min(c, last)) * block, block)
                if c <= last:
                    stage_ref[staged, :] = value[
                        n * block : (n + 1) * block, c * 128 : (c + 1) * 128
                    ]
                there = pl.ds(pl.multiple_of(place + c * stride + k * rows, 16), block)
                at = (n * 2 + k) * places + c
                stores.append(
                    pltpu.make_async_copy(stage_ref.at[staged], part_hbm.at[there], sem.at[at])
                )
                stores[-1].start()

    xf = x.astype(F32)
    logit = jnp.sum(xf * router, axis=1, keepdims=True)
    gate = 1.0 / (1.0 + jnp.exp(-logit))
    first, second = weights()
    pre = jnp.dot(x, first, preferred_element_type=F32)
    hidden_grad = nt(g, second)
    tanh_value = jnp.tanh(tanh_scale * (pre + cubic_term * pre * pre * pre))
    act = 0.5 * pre * (1.0 + tanh_value)
    scaled_act = (act * gate).astype(BF)
    send(jnp.dot(scaled_act, second, preferred_element_type=F32).astype(BF), 0)
    slope = 0.5 * (1.0 + tanh_value) + 0.5 * pre * (
        1.0 - tanh_value * tanh_value
    ) * tanh_scale * (1.0 + 3.0 * cubic_term * pre * pre)
    gate_grad = jnp.sum(act * hidden_grad, axis=1, keepdims=True)
    logit_grad = gate_grad * gate * (1.0 - gate)
    pre_grad = (hidden_grad * gate * slope).astype(BF)
    send((nt(pre_grad, first) + logit_grad * router).astype(BF), 1)
    hidden = pre_grad.shape[1]
    kept_ref[:, 0:hidden] = pre_grad
    kept_ref[:, hidden:] = scaled_act
    return jnp.sum(xf * logit_grad, axis=0, keepdims=True)


def own_kernel(
    stride, index_ref, msg_ref, first_hbm, second_hbm, router_ref,
    part_hbm, kept_ref, sum_ref, first_ref, second_ref,
    x_ref, g_ref, stage_ref, sem, load_sem,
):
    loads = [
        pltpu.make_async_copy(first_hbm, first_ref, load_sem.at[0]),
        pltpu.make_async_copy(second_hbm, second_ref, load_sem.at[1]),
    ]
    for load in loads:
        load.start()
    stores = []

    def weights():
        for load in loads:
            load.wait()
        return first_ref[...], second_ref[...]

    sum_ref[...] = expert_block(
        PARTS * x_ref.shape[0], stride, index_ref, [(0, msg_ref)], weights, router_ref,
        (part_hbm, kept_ref, x_ref, g_ref, stage_ref, sem), stores,
    )
    for store in stores:
        store.wait()


def rest_kernel(
    stride, index_ref, up_ref, down_ref, first_ref, second_ref, router_ref, before_ref, _,
    part_hbm, kept_ref, x_ref, g_ref, stage_ref, tail_ref, sem, tail_sem,
):
    rows = PARTS * x_ref.shape[0] // 2
    stores = []
    router_sum = before_ref[...] + expert_block(
        rows, stride, index_ref, [(2, up_ref), (1, down_ref)],
        lambda: (first_ref[...], second_ref[...]), router_ref,
        (part_hbm, kept_ref, x_ref, g_ref, stage_ref, sem), stores,
    )
    tail = stride - 2 * rows
    last = x_ref.shape[1] // 128 - 1
    total = part_hbm.shape[0]
    for c in range(-(-total // stride)):
        if c <= last:
            row = jnp.where(
                iota((tail, 128), 0) == 0, router_sum[:, c * 128 : (c + 1) * 128], 0.0
            )
            tail_ref[pl.ds(c * tail, tail), :] = row.astype(BF)
        start = c * stride + 2 * rows
        size = min(tail, total - start)
        stores.append(
            pltpu.make_async_copy(
                tail_ref.at[pl.ds(min(c, last) * tail, size)],
                part_hbm.at[pl.ds(start, size)],
                tail_sem.at[c],
            )
        )
        stores[-1].start()
    for store in stores:
        store.wait()


def weight_kernel(
    own_hbm, up_hbm, down_hbm, own_ref, rest_ref,
    first_ref, second_ref, msg_ref, x_ref, g_ref, sem,
):
    loads = fetch((own_hbm, up_hbm, down_hbm), msg_ref, sem)
    for load in loads:
        load.start()
    sort = sorting()
    for k, load in enumerate(loads):
        load.wait()
        unpack(sort, msg_ref, k, x_ref, g_ref)
    kept = jnp.concatenate([own_ref[...], rest_ref[...]], axis=0)
    pre_grad, scaled_act = jnp.split(kept, 2, axis=1)
    first_ref[...] = tn(x_ref[...], pre_grad).astype(BF)
    second_ref[...] = tn(scaled_act, g_ref[...]).astype(BF)


def return_kernel(rows, shift_ref, sum_ref, msg_ref, hold_ref):
    depth = hold_ref.shape[0]
    given = sum_ref.shape[0]
    base = given // 16 * 16
    hold_ref[pl.ds(base, depth - base), :] = jnp.zeros((depth - base, 128), BF)
    hold_ref[pl.ds(0, given), :] = sum_ref[...]
    shift = shift_ref[0]
    held = hold_ref[...]
    block = 256
    for b in range(msg_ref.shape[0] // block):
        row = iota((block, depth), 0) + b * block
        source = lax.shift_right_logical(row, 4)
        r = row & 15
        slot = jnp.where(r < 6, r, r - 6)
        want = lax.shift_right_logical(slot, 1) * (rows // PARTS) + source * 2 + (slot & 1)
        want = jnp.where(r < 6, want, rows + want)
        want = jnp.where(r < 12, want, jnp.where(r == 12, 2 * rows, -depth)) + shift
        msg_ref[pl.ds(b * block, block), :] = jnp.dot(
            one(want == iota((block, depth), 1)), held, preferred_element_type=F32
        ).astype(BF)


def collect_kernel(code_ref, msg_ref, out_ref):
    held = msg_ref[...]
    depth = held.shape[0]
    tok_rows = code_ref.shape[1]
    picked = None
    for m in range(2):
        code = to_column(code_ref[m : m + 1, :])
        want = (lax.shift_right_logical(code, 3) * 2 + m) * 16 + (code & 7)
        lane = iota((tok_rows, depth), 1)
        out_ref[pl.ds(m * tok_rows, tok_rows), :] = jnp.dot(
            one(lane == want), held, preferred_element_type=F32
        ).astype(BF)
        pick = one(lane == want + 6)
        picked = pick if picked is None else picked + pick
    out_ref[pl.ds(2 * tok_rows, tok_rows), :] = jnp.dot(picked, held, preferred_element_type=F32).astype(BF)
    n = depth // 16
    row = iota((n, depth), 0)
    want = ((row & (n // 2 - 1)) * 2 + jnp.where(row >= n // 2, 1, 0)) * 16 + 12
    out_ref[pl.ds(3 * tok_rows, n), :] = jnp.dot(
        one(iota((n, depth), 1) == want), held, preferred_element_type=F32
    ).astype(BF)


def final_kernel(part_ref, own_ref, up_ref, down_ref, moe_hbm, token_ref, router_ref, sem):
    tok_rows, width = token_ref.shape
    pieces = []
    for ref, shift in ((own_ref, 0), (up_ref, 2), (down_ref, 1)):
        part = wrap(part_ref[0] + shift)
        for k in range(up_ref.shape[0]):
            lanes = pl.ds(pl.multiple_of((part + PARTS * k) * 128, 128), 128)
            pieces.append((ref.at[k], lanes))
    pieces.append((own_ref.at[own_ref.shape[0] - 1], pl.ds(width - 128, 128)))
    stores = []
    for k, (block, lanes) in enumerate(pieces):
        stores.append(
            pltpu.make_async_copy(
                block.at[pl.ds(0, 2 * tok_rows)], moe_hbm.at[:, lanes], sem.at[k]
            )
        )
        stores[-1].start()
    for block, lanes in pieces:
        token_ref[:, lanes] = block[2 * tok_rows : 3 * tok_rows, :].astype(F32)
        router_ref[:, lanes] = block[3 * tok_rows :, :].astype(F32)
    for store in stores:
        store.wait()


def call(kernel, out, specs, name, flops, size, scratch=(), out_specs=None, limit=FULL, alias=None):
    return pl.pallas_call(
        kernel,
        out_shape=[jax.ShapeDtypeStruct(s, d) for s, d in out],
        in_specs=specs,
        out_specs=out_specs or [VM] * len(out),
        scratch_shapes=list(scratch),
        input_output_aliases=alias or {},
        compiler_params=pltpu.CompilerParams(vmem_limit_bytes=limit),
        cost_estimate=pl.CostEstimate(flops=flops, bytes_accessed=size, transcendentals=0),
        name=name,
    )


def shards(tokens, route_ids, router, w_in, w_out, out_grad):
    members, tok_rows = route_ids.shape[0], route_ids.shape[1]
    experts, width = router.shape[2], router.shape[1]
    hidden = w_in.shape[3]
    places = experts * members
    capacity = 3 * tok_rows // (2 * experts)
    rows = places * capacity
    half = width // 2
    plane = ("dp", "member")
    z_count = lax.axis_size("expert")
    z = lax.axis_index("expert")
    part_index = (z % PARTS).reshape(1)
    ahead = [(k, (k + 1) % z_count) for k in range(z_count)]
    behind = [(k, (k - 1) % z_count) for k in range(z_count)]
    lines = [list(range(k, z_count, PARTS)) for k in range(PARTS)]

    dma = pltpu.SemaphoreType.DMA
    msg, codes = call(
        dispatch_kernel,
        [((experts, members, 8, half), BF), ((members, tok_rows), jnp.int32)],
        [SM] + [HB] * 3, "dispatch", 3 << 30, 4 << 20,
        scratch=[
            pltpu.VMEM((members, tok_rows), jnp.int32),
            pltpu.VMEM((tok_rows, width), BF),
            pltpu.VMEM((members, tok_rows, width), BF),
            pltpu.VMEM((experts, members, 8, half), BF),
            dma((4,)),
            dma((2,)),
        ],
        out_specs=[HB, VM],
    )(part_index, route_ids[:, :, 0], tokens, out_grad)
    own = lax.all_to_all(
        msg.reshape(places, 8, half), plane, split_axis=0, concat_axis=0, tiled=True
    ).reshape(places * 8, half)
    arrived = (own, lax.ppermute(own, "expert", ahead), lax.ppermute(own, "expert", behind))
    column = lax.dynamic_slice(
        router, (lax.axis_index("member"), 0, lax.axis_index("dp")), (1, width, 1)
    ).reshape(1, width)
    stride = 2 * rows + 32
    share = stride - 2
    block = rows // PARTS
    chunks = width // 128
    whole = ((z_count * share, 128), BF)
    side = pltpu.VMEM((block, width), BF)
    part, kept_own, router_own, first, second = call(
        functools.partial(own_kernel, stride),
        [
            whole,
            ((block, 2 * hidden), BF),
            ((1, width), F32),
            ((width, hidden), BF),
            ((hidden, width), BF),
        ],
        [SM, VM, HB, HB, VM], "expert_own", 1 << 30, 6 << 20,
        scratch=[
            side,
            side,
            pltpu.VMEM((2 * chunks * block, 128), BF),
            dma((2 * z_count,)),
            dma((2,)),
        ],
        out_specs=[HB] + [VM] * 4, limit=MOST,
    )(part_index, own, w_in[0, 0], w_out[0, 0], column)
    sides = pltpu.VMEM((2 * block, width), BF)
    part, kept_rest = call(
        functools.partial(rest_kernel, stride),
        [whole, ((2 * block, 2 * hidden), BF)],
        [SM] + [VM] * 6 + [HB], "expert_rest", 2 << 30, 8 << 20,
        scratch=[
            sides,
            sides,
            pltpu.VMEM((4 * chunks * block, 128), BF),
            pltpu.VMEM((chunks * (stride - 2 * rows), 128), BF),
            dma((4 * z_count,)),
            dma((z_count,)),
        ],
        out_specs=[HB, VM], limit=MOST, alias={7: 0},
    )(part_index, *arrived[1:], first, second, column, router_own, part)
    total = lax.psum_scatter(part, "expert", scatter_dimension=0, tiled=True)
    (back,) = call(
        functools.partial(return_kernel, rows),
        [((places * 16, 128), BF)],
        [SM, VM], "to_tokens", 1 << 28, 1 << 20,
        scratch=[pltpu.VMEM((-(-share // 128) * 128, 128), BF)],
        limit=LIMIT,
    )(2 * z.reshape(1), total)
    home = lax.all_to_all(
        back.reshape(places, 16, 128), plane, split_axis=0, concat_axis=0, tiled=True
    ).reshape(places * 16, 128)
    grad_first, grad_second = call(
        weight_kernel,
        [((width, hidden), BF), ((hidden, width), BF)],
        [HB] * 3 + [VM] * 2, "weights", 1 << 30, 6 << 20, limit=LESS,
        scratch=[pltpu.VMEM((rows * 4, half), BF)]
        + [pltpu.VMEM((rows, width), BF)] * 2
        + [dma((2 * PARTS,))],
    )(*arrived, kept_own, kept_rest)
    (compact,) = call(
        collect_kernel,
        [(((members + 1) * tok_rows + places, 128), BF)],
        [VM] * 2, "collect", 1 << 28, 1 << 20, limit=LIMIT,
    )(codes, home)
    line = lax.all_gather(compact, "expert", axis_index_groups=lines)
    moe, token_grad, router_rows = call(
        final_kernel,
        [((members * tok_rows, width), BF), ((tok_rows, width), F32), ((places, width), F32)],
        [SM] + [VM] * 3, "final", 1 << 20, 4 << 20, limit=LIMIT,
        scratch=[dma((chunks,))], out_specs=[HB, VM, VM],
    )(
        part_index,
        line,
        lax.ppermute(line[:-1], "expert", ahead),
        lax.ppermute(line[:-1], "expert", behind),
    )
    router_grad = jnp.transpose(router_rows.reshape(members, experts, width), (0, 2, 1))
    return (
        moe.reshape(members, tok_rows, width),
        token_grad,
        grad_first[None, None],
        grad_second[None, None],
        router_grad,
    )


def solution(mesh):
    in_specs = (
        P(("dp", "member"), None),
        P(None, ("dp", "member"), None),
        P(),
        P("member", "dp", None, "expert"),
        P("member", "dp", "expert", None),
        P(None, ("dp", "member"), None),
    )
    out_specs = (
        P(None, ("dp", "member"), None),
        P(("dp", "member"), None),
        P("member", "dp", None, "expert"),
        P("member", "dp", "expert", None),
        P(),
    )
    return jax.shard_map(shards, mesh=mesh, in_specs=in_specs, out_specs=out_specs, check_vma=False)
```
